32 devices in a mesh: mesh: 16 (over z, x, core), band: 2 (over y).
Axes of the slice: x: 2, y: 2, z: 4, core: 2. Of those that a mesh axis runs over, the one named last changes fastest.
Arguments:
- band_block: bfloat16 [320, 4096], P('band', 'mesh'), may hold values from -6 to 6
- band_basis: bfloat16 [4096, 3072], P('mesh', 'band'), may hold values from -0.25 to 0.25
- mass_scale: float32 [4096], P('mesh'), may hold values from 0.7 to 1.5
- cell_matrices: bfloat16 [256, 4096], P('mesh')
- cell_nodes: int32 [256, 64], P('mesh'), may hold values from 0 to 319, as said below
- cell_count: int32 [16], P('mesh'), may hold values from 8 to 16, as said below
- send_index: int32 [16, 4, 16], P('mesh'), may hold values from 0 to 256, as said below
Outputs:
- filtered: bfloat16 [320, 4096], P('band', 'mesh')
- intersection: float32 [3072, 320], P('mesh', 'band')
- hamiltonian: float32 [3072, 320], P('mesh', 'band')
The draws below stay inside these ranges and needn't reach their ends.
Inputs may be any that keep to these rules, and one draw needn't show every extreme that they name: `cell_nodes`: an entry below 256 is an owned node of the cell's partition; an entry 256 + k * 16 + c names ghost c of neighbour slot k, and c is always below the number of nodes that neighbour lists for this partition. In some partition the first cell's first entry is the last ghost slot, 319. send_index[p, k, :] lists, in ghost-slot order, owned nodes of partition p held by the partition (p + off(k)) mod 16; used slots come first and 256 marks an unused slot. Only partitions within 2 index steps (cyclically) share nodes. Some partition lists 16 nodes toward every neighbour and receives 16 from every neighbour. `cell_count`: some partition has all 16 cells live.
All inputs are finite; a program needn't handle non-finite values.
Results may differ from the reference program's by a relative error of at most 0.012.
Values may be sent and summed in bfloat16 or wider, within the bound.
A program may use at most 64 MiB of HBM per device.

```python
import math
import jax
import jax.numpy as jnp
from jax import lax

BANDS = 3072
NPC = 64
REACH = 2
NODES_DEV = 256
CELLS_DEV = 16
SLOTS = 16
PARTS_SIZE = 16
NODES = 4096
BLOCKS = 320


def slot_offsets():
    slot_index = jnp.arange(2 * REACH, dtype=jnp.int32)
    offsets = jnp.where(slot_index < REACH, slot_index + 1, REACH - 1 - slot_index).astype(jnp.int32)
    partners = ((slot_index + REACH) % (2 * REACH)).astype(jnp.int32)
    return (offsets, partners)


def slot_counts(key):
    base = jax.random.fold_in(key, 71)
    first_key, second_key = jax.random.split(base)
    counts = jax.random.randint(first_key, (PARTS_SIZE, 2 * REACH), SLOTS // 2, SLOTS + 1)
    chosen = jax.random.randint(second_key, (), 0, PARTS_SIZE)
    offsets, partners = slot_offsets()
    owners = jnp.arange(PARTS_SIZE, dtype=jnp.int32)[:, None]
    target = (owners + offsets[None, :]) % PARTS_SIZE
    full = jnp.logical_or(target == chosen, owners == chosen)
    return (jnp.where(full, SLOTS, counts).astype(jnp.int32), chosen)


def draw_send_index(key, part):
    counts, chosen = slot_counts(key)
    picks = jax.random.randint(jax.random.fold_in(key, 5), (PARTS_SIZE, 2 * REACH, SLOTS), 0, NODES_DEV)
    position = jnp.arange(SLOTS, dtype=jnp.int32)[None, None, :]
    return jnp.where(position < counts[:, :, None], picks, NODES_DEV).astype(jnp.int32)


def draw_cell_nodes(key, part):
    counts, chosen = slot_counts(key)
    offsets, partners = slot_offsets()
    owners = jnp.arange(PARTS_SIZE, dtype=jnp.int32)[:, None]
    incoming = counts[(owners + offsets[None, :]) % PARTS_SIZE, partners[None, :]]
    keys = jax.random.split(jax.random.fold_in(key, 9), 4)
    shape = (PARTS_SIZE, CELLS_DEV, NPC)
    is_ghost = jax.random.randint(keys[0], shape, 0, 5) == 0
    neighbour = jax.random.randint(keys[1], shape, 0, 2 * REACH)
    raw_pos = jax.random.randint(keys[2], shape, 0, 1 << 20)
    owned = jax.random.randint(keys[3], shape, 0, NODES_DEV)
    part_ids = jnp.arange(PARTS_SIZE, dtype=jnp.int32)[:, None, None]
    limit = incoming[part_ids, neighbour]
    ghost_value = NODES_DEV + neighbour * SLOTS + raw_pos % limit
    nodes = jnp.where(is_ghost, ghost_value, owned).astype(jnp.int32)
    nodes = nodes.at[chosen, 0, 0].set(NODES_DEV + 2 * REACH * SLOTS - 1)
    nodes = nodes.at[chosen, 0, 1].set(0)
    return nodes.reshape(PARTS_SIZE * CELLS_DEV, NPC)


def draw_cell_count(key, part):
    first_key, second_key = jax.random.split(jax.random.fold_in(key, 13))
    counts = jax.random.randint(first_key, (PARTS_SIZE,), CELLS_DEV // 2, CELLS_DEV + 1)
    chosen = jax.random.randint(second_key, (), 0, PARTS_SIZE)
    counts = counts.at[chosen].set(CELLS_DEV)
    counts = counts.at[(chosen + 1) % PARTS_SIZE].set(CELLS_DEV // 2)
    return counts.astype(jnp.int32)


def draw_cell_matrices(key, part):
    shape = (PARTS_SIZE * CELLS_DEV, NPC, NPC)
    entries = jax.random.normal(key, shape, jnp.float32)
    symmetric = (entries + jnp.swapaxes(entries, 1, 2)) * (0.5 / math.sqrt(2.0 * NPC))
    return symmetric.reshape(PARTS_SIZE * CELLS_DEV, NPC * NPC).astype(jnp.bfloat16)


def strengthened(values, key, source, target, parts, factor):
    owner, partner = [(jnp.arange(values.shape[axis_at]) // (values.shape[axis_at] // parts)).reshape([-1 if axis == axis_at else 1 for axis in range(values.ndim)]) for axis_at in (source, target)]
    chosen = jax.random.permutation(key, parts)[partner]
    strong = (owner == chosen) | (owner == (partner + parts // 2) % parts)
    return jnp.where(strong, factor * values, values)


def block_scale(own_key, extent, cuts, smallest, high):
    def one(dim, shards_of):
        steps = jax.random.uniform(jax.random.fold_in(jax.random.fold_in(own_key, 6), dim), (shards_of,), jnp.float32, smallest / len(cuts), high / len(cuts))
        return jnp.repeat(jnp.exp(steps), extent[dim] // shards_of).reshape((-1,) + (1,) * (len(extent) - dim - 1))

    gain = one(*cuts[0])
    for cut in cuts[1:]:
        gain = gain * one(*cut)
    return gain


def gaussian(stream_key, shape, scale, most, cuts=(), kind=jnp.bfloat16):
    level = block_scale(stream_key, shape, cuts, -0.22, 0.18) if cuts else 1.0
    result = jax.random.normal(stream_key, shape, jnp.float32) * scale * level
    return jnp.minimum(jnp.maximum(result, -most), most).astype(kind)


def noise_with(stream_key, extent, scale, most, shards, heavy, held_as=jnp.bfloat16):
    array = scale * jax.random.normal(stream_key, extent, jnp.float32)
    if shards:
        array = array * block_scale(stream_key, extent, shards, -0.22, 0.18)
    return jnp.clip(strengthened(array, jax.random.fold_in(stream_key, 3), *heavy), -most, most).astype(held_as)


def setup_inputs(seed: int = 0) -> dict:
    splits = jax.random.split(jax.random.key(seed), 8)
    band_block = gaussian(splits[0], (BLOCKS, NODES), 1.0, 6.0, ((0, 2), (1, 16)))
    band_basis = noise_with(splits[1], (NODES, BANDS), (NODES // 4) ** -0.5, 0.25, ((0, 16), (1, 2)), (0, 1, 16, 2.0))
    mass_scale = jnp.clip(jnp.exp(math.log(1.5) - 0.7621401 * jax.random.uniform(splits[2], (NODES,), jnp.float32) ** block_scale(splits[2], (NODES,), ((0, 16),), -0.2, 0.2)), 0.7, 1.5)
    cell_matrices = draw_cell_matrices(jax.random.fold_in(splits[7], 71), 0)
    cell_nodes = draw_cell_nodes(jax.random.fold_in(splits[7], 71), 0)
    cell_count = draw_cell_count(jax.random.fold_in(splits[7], 71), 0)
    send_index = draw_send_index(jax.random.fold_in(splits[7], 71), 0)
    return {"band_block": band_block, "band_basis": band_basis, "mass_scale": mass_scale, "cell_matrices": cell_matrices, "cell_nodes": cell_nodes, "cell_count": cell_count, "send_index": send_index}


filter_centre = 1.5
filter_half = 2.5
first_sigma = -0.625


def sigma_values():
    values = [first_sigma]
    for _ in range(2):
        values.append(1.0 / (2.0 / first_sigma - values[-1]))
    return values


def global_node_ids(cell_nodes, send_index):
    width = 2 * REACH
    slot_index = jnp.arange(width, dtype=jnp.int32)
    offsets = jnp.where(slot_index < REACH, slot_index + 1, REACH - 1 - slot_index).astype(jnp.int32)
    partners = ((slot_index + REACH) % width).astype(jnp.int32)
    local_ids = cell_nodes.reshape(PARTS_SIZE, CELLS_DEV, NPC)
    owner_part = jnp.arange(PARTS_SIZE, dtype=jnp.int32)[:, None, None]
    ghost_pos = jnp.maximum(local_ids - NODES_DEV, 0)
    neighbour = jnp.minimum(ghost_pos // SLOTS, width - 1)
    position = ghost_pos % SLOTS
    source = (owner_part + offsets[neighbour]) % PARTS_SIZE
    remote = send_index[source, partners[neighbour], position]
    return jnp.where(local_ids < NODES_DEV, owner_part * NODES_DEV + local_ids, source * NODES_DEV + remote).astype(jnp.int32)


def reference(band_block, band_basis, mass_scale, cell_matrices, cell_nodes, cell_count, send_index):
    node_ids = global_node_ids(cell_nodes, send_index)
    live_mask = (jnp.arange(CELLS_DEV, dtype=jnp.int32)[None, :] < cell_count[:, None]).astype(jnp.float32)
    matrices = cell_matrices.reshape(PARTS_SIZE, CELLS_DEV, NPC, NPC)
    columns = band_block.shape[0]

    def operate(field):
        scaled = (mass_scale[None, :] * field.astype(jnp.float32)).astype(jnp.bfloat16)

        def one_part(summed, inputs):
            part_ids, part_mats, part_live = inputs
            gathered = scaled[:, part_ids].astype(jnp.float32)
            products = jnp.einsum("cij,bcj->bci", part_mats.astype(jnp.float32), gathered)
            products = products * part_live[None, :, None]
            summed = summed.at[:, part_ids.reshape(-1)].add(products.reshape(columns, -1))
            return summed, None

        summed, _ = lax.scan(one_part, jnp.zeros((columns, NODES), jnp.float32), (node_ids, matrices, live_mask))
        return mass_scale[None, :] * summed

    sigmas = sigma_values()
    previous = band_block
    applied = operate(band_block)
    current = ((applied - filter_centre * band_block.astype(jnp.float32)) * (sigmas[0] / filter_half)).astype(jnp.bfloat16)
    for step in range(1, 3):
        applied = operate(current)
        scale_now = 2.0 * sigmas[step] / filter_half
        mixing = sigmas[step - 1] * sigmas[step]
        update = (applied - filter_centre * current.astype(jnp.float32)) * scale_now - mixing * previous.astype(jnp.float32)
        previous = current
        current = update.astype(jnp.bfloat16)
    filtered = current
    image = operate(filtered).astype(jnp.bfloat16)
    dims = (((0,), (1,)), ((), ()))
    intersection = lax.dot_general(band_basis, filtered, dims, preferred_element_type=jnp.float32)
    hamiltonian = lax.dot_general(band_basis, image, dims, preferred_element_type=jnp.float32)
    return filtered, intersection, hamiltonian
```

```python
import functools
import math
import jax
import jax.numpy as jnp
from jax import lax
from jax.experimental import pallas as pl
from jax.experimental.pallas import tpu as pltpu
from jax.sharding import PartitionSpec as P

filter_centre = 1.5
filter_half = 2.5
first_sigma = -0.625
MESH = pl.DeviceIdType.MESH
bf16 = jnp.bfloat16
f32 = jnp.float32


def sigma_values():
    values = [first_sigma]
    for _ in range(2):
        values.append(1.0 / (2.0 / first_sigma - values[-1]))
    return values


def neighbour_offset(neighbour, reach):
    if neighbour < reach:
        return neighbour + 1
    return reach - 1 - neighbour


def dot(a, b):
    return jnp.dot(a, b, preferred_element_type=f32)


def dot_nt(a, b):
    return lax.dot_general(a, b, (((1,), (1,)), ((), ())), preferred_element_type=f32)


def routes(reach, slots):
    width = 2 * reach
    offs = [neighbour_offset(k, reach) for k in range(width)]
    found, row = [], 0
    for d in [*range(1, width + 1), *range(-1, -width - 1, -1)]:
        pieces = []
        for k in range(width):
            if offs[k] == d:
                pieces += [("own", k, 0), ("back", k, 0)]
            pieces += [("third", k, j) for j in range(width) if offs[k] + offs[j] == d]
        found.append((d, row, [(row + slots * i, *piece) for i, piece in enumerate(pieces)]))
        row += slots * len(pieces)
    return found, row


def kernel(
    n, nb, group, packed, folded, x_ref, basis_ref, mass_ref, mats_ref, nodes_ref, count_ref, send_ref,
    f_ref, inter_ref, ham_ref,
    full, block, perm, ghost_out, ghost_in, mats, hots, coupled, stiff, stack, intro_out, intro, out, landed,
    held, edge, summed, tile, across, merged, got,
    block_sem, intro_send, intro_recv, halo_send, halo_recv, gb_send, gb_recv, basis_send, basis_recv,
    held_send, held_recv, edge_send, edge_recv,
    cross_send, cross_recv, tile_send, tile_recv,
):
    me = lax.axis_index("mesh")
    mine = lax.axis_index("band")
    seat = lax.rem(me, group)
    team = me // group
    teams = n // group
    folds = math.gcd(2, teams)
    lines = teams // folds
    line, side = team // folds, lax.rem(team, folds)
    columns, owned = x_ref.shape
    width, slots = send_ref.shape[1:]
    reach = width // 2
    rows = inter_ref.shape[1]
    per_band = n // nb
    per_seat = per_band // group
    ghosts = width * slots
    total = owned + ghosts
    cells, corners = nodes_ref.shape
    wide = intro.shape[1]
    plan, sent = routes(reach, slots)

    barrier = pltpu.get_barrier_semaphore()

    def greet(d, carry):
        pl.semaphore_signal(
            barrier, inc=1, device_id=(lax.rem(me + d, n), mine), device_id_type=MESH
        )
        return carry

    lax.fori_loop(1, n, greet, 0)
    for d in range(1, nb):
        for e in range(group):
            pl.semaphore_signal(
                barrier,
                inc=1,
                device_id=(team * group + lax.rem(seat + e, group), lax.rem(mine + d, nb)),
                device_id_type=MESH,
            )

    load = pltpu.make_async_copy(basis_ref, block, block_sem)
    load.start()

    def remote(source, target, send, recv, device):
        return pltpu.make_async_remote_copy(
            src_ref=source, dst_ref=target, send_sem=send, recv_sem=recv,
            device_id=device, device_id_type=MESH,
        )

    def partition(d):
        return (lax.rem(me + d + n, n), mine)

    def beside(e, d):
        return (team * group + lax.rem(seat + e, group), lax.rem(mine + d, nb))

    parts = (pl.ds(0, owned), pl.ds(owned, ghosts))
    ready = (perm, ghost_in)

    def basis_copy(part, e, d):
        source = ready[part].at[lax.rem(seat + e, group)]
        target = full.at[seat, mine, parts[part]]
        if e == 0 and d == 0:
            return pltpu.make_async_copy(source, target, basis_recv.at[part, e, d])
        return remote(source, target, basis_send.at[part, e, d], basis_recv.at[part, e, d], beside(e, d))

    def basis_wait(part, e, d):
        if e == 0 and d == 0:
            basis_copy(part, e, d).wait()
            return
        target = full.at[lax.rem(seat + group - e, group), lax.rem(mine + nb - d, nb), parts[part]]
        remote(ready[part].at[0], target, basis_send.at[part, e, d], basis_recv.at[part, e, d],
               beside(e, d)).wait_recv()

    places = [(e, d) for d in [*range(1, nb), 0] for e in range(group)]

    def basis_out(part):
        for e, d in places:
            if e == 0 and d == 0:
                basis_copy(part, e, d).start()
            else:
                launch([basis_copy(part, e, d)])

    owned_ids = lax.broadcasted_iota(jnp.int32, (owned, slots), 0)
    hot_parts = [
        jnp.where(owned_ids == send_ref[0, k : k + 1, :], 1.0, 0.0) for k in range(width)
    ]
    send_hot_f = jnp.concatenate(hot_parts, axis=1)
    send_hot_t = send_hot_f.astype(bf16)
    send_hot = send_hot_f.T.astype(bf16)

    mass_row = mass_ref[...]
    high = mass_row.astype(bf16).astype(f32)
    middle = (mass_row - high).astype(bf16).astype(f32)
    low = mass_row - high - middle
    level = lax.broadcasted_iota(jnp.int32, (8, owned), 0)
    extra = jnp.where(level == 0, high, jnp.where(level == 1, middle, jnp.where(level == 2, low, 0.0)))
    raised = jnp.concatenate(
        [x_ref[...].astype(f32), extra, jnp.zeros((wide - columns - 8, owned), f32)], axis=0
    ).T.astype(bf16)
    first_id = columns + 3
    lane = lax.broadcasted_iota(jnp.int32, (ghosts, wide), 1)
    message = dot(send_hot, raised)
    numbers = dot(
        send_hot, (lax.broadcasted_iota(jnp.int32, (owned, wide), 0) + 1).astype(f32).astype(bf16)
    )
    for j in range(width):
        tiled = jnp.concatenate([numbers[j * slots : (j + 1) * slots]] * width, axis=0)
        message = jnp.where(lane == first_id + j, tiled, message)
    intro_out[...] = message.astype(bf16)
    mass_own = jnp.broadcast_to(mass_row, (8, owned)).T[:, :1]

    load.wait()
    for s in range(group):
        starts = [(s + group * t) * rows for t in range(per_seat)]
        perm[s] = jnp.concatenate([block[:, a : a + rows] for a in starts], axis=1)
        ghost_out[s] = dot(send_hot, perm[s]).astype(bf16)

    pl.semaphore_wait(barrier, n - 1 + (nb - 1) * group)

    def halo(source, target, send, recv, cut):
        return [
            remote(cut(source, k), cut(target, (k + reach) % width), send.at[k], recv.at[(k + reach) % width],
                   partition(neighbour_offset(k, reach)))
            for k in range(width)
        ]

    started = []

    def launch(copies):
        for copy in copies:
            copy.start()
        started.extend(copies)

    intros = halo(intro_out, intro, intro_send, intro_recv, lambda ref, k: ref.at[pl.ds(k * slots, slots)])
    launch(intros)
    rims = halo(ghost_out, ghost_in, gb_send, gb_recv, lambda ref, k: ref.at[:, pl.ds(k * slots, slots)])
    launch(rims)
    def after_send(index):
        if index == 0:
            basis_out(0)
        if index == 1:
            for copy in rims:
                copy.wait_recv()
            basis_out(1)

    after_send(0)

    fold = 128 // corners
    strips = corners // fold
    stacked = jnp.concatenate([mats_ref[:, a * 128 : (a + 1) * 128] for a in range(strips)], axis=0)
    row = lax.broadcasted_iota(jnp.int32, (cells * corners, cells * strips), 0)
    column = lax.broadcasted_iota(jnp.int32, (cells * corners, cells * strips), 1)
    picked = (row % corners) // fold * cells + row // corners == column
    spread = dot(jnp.where(picked, 1.0, 0.0).astype(bf16), stacked)
    turn = lax.broadcasted_iota(jnp.int32, (cells * corners, corners), 0) % fold
    unfolded = spread[:, :corners]
    for a in range(1, fold):
        unfolded = jnp.where(turn == a, spread[:, a * corners : (a + 1) * corners], unfolded)
    mats[...] = unfolded.astype(bf16)

    live = count_ref[0]
    total_ids = lax.broadcasted_iota(jnp.int32, (total, corners), 0)
    for c in range(cells):
        hot = jnp.where(
            jnp.logical_and(total_ids == nodes_ref[c : c + 1, :], c < live), 1.0, 0.0
        ).astype(bf16)
        part = slice(c * corners, (c + 1) * corners)
        hots[:, part] = hot
        coupled[:, part] = dot_nt(hot, mats[part, :]).astype(bf16)
    stiff[...] = dot_nt(hots[...], coupled[...]).astype(bf16)

    own_rows = dot(send_hot, stiff[:owned, :]).astype(bf16)
    for _, _, pieces in plan:
        for row, kind, k, _ in pieces:
            if kind == "own":
                stack[row : row + slots, :] = own_rows[k * slots : (k + 1) * slots]
            if kind == "back":
                stack[row : row + slots, :] = stiff[owned + k * slots : owned + (k + 1) * slots, :]
    stack[sent + ghosts :, :] = stiff[:owned, :]

    for copy in intros:
        copy.wait_recv()
    there = intro[...].astype(f32)
    turned = there.T
    mass_ghost = there[:, columns : columns + 1] + there[:, columns + 1 : columns + 2] + there[:, columns + 2 : columns + 3]
    mass = jnp.concatenate([mass_own, mass_ghost], axis=0)
    slot_lane = lax.broadcasted_iota(jnp.int32, (1, ghosts), 1)
    listed = jnp.zeros((1, ghosts), f32)
    for k in range(width):
        at = first_id + (k + reach) % width
        inside = jnp.logical_and(slot_lane >= k * slots, slot_lane < (k + 1) * slots)
        listed = jnp.where(inside, turned[at : at + 1, :], listed)
    piece_lane = lax.broadcasted_iota(jnp.int32, (slots, ghosts), 1)
    mixers = []
    for k in range(width):
        inside = jnp.logical_and(piece_lane >= k * slots, piece_lane < (k + 1) * slots)
        for j in range(width):
            column = there[k * slots : (k + 1) * slots, first_id + j : first_id + j + 1]
            mixers.append(jnp.where(jnp.logical_and(inside, column == listed), 1.0, 0.0))
    mixed = dot(jnp.concatenate(mixers, axis=0).astype(bf16), stiff[owned:, :]).astype(bf16)

    def mixed_rows(k, j):
        return mixed[(k * width + j) * slots : (k * width + j + 1) * slots]

    for _, _, pieces in plan:
        for row, kind, k, j in pieces:
            if kind == "third":
                stack[row : row + slots, :] = mixed_rows(k, j)
    for k in range(width):
        stack[sent + k * slots : sent + (k + 1) * slots, :] = mixed_rows(k, (k + reach) % width)

    def held_copies(which, e, owner):
        return [
            remote(ref.at[which, owner], ref.at[which, owner], send.at[which, e], recv.at[which, e], beside(e, 0))
            for ref, send, recv in ((held, held_send, held_recv), (edge, edge_send, edge_recv))
        ]

    def share_field(which, inner, outer):
        held[which, seat] = inner.T.astype(bf16)
        outer = outer.T
        if folded:
            outer = jnp.concatenate([outer[: columns // 2], outer[columns // 2 :]], axis=1)
        edge[which, seat] = outer.astype(bf16)
        for e in range(1, group):
            launch(held_copies(which, e, seat))

    def field(which, i):
        outer = edge[which, i]
        if folded:
            outer = jnp.concatenate([outer[:, :ghosts], outer[:, ghosts:]], axis=0)
        return jnp.concatenate([held[which, i], outer], axis=1)

    def pack(value):
        if not packed:
            return value
        half = columns // 2
        left = rows - rows % 128
        rest = jnp.concatenate([value[:half, left:], value[half:, left:]], axis=1)
        parts = [value[:, a : a + 128] for a in range(0, left, 128)]
        return jnp.concatenate(parts + [rest], axis=0)

    def unpack(value):
        if not packed:
            return value
        full_parts = rows // 128
        parts = [value[a * columns : (a + 1) * columns] for a in range(full_parts)]
        rest = value[full_parts * columns :]
        parts.append(jnp.concatenate([rest[:, :64], rest[:, 64:]], axis=0))
        return jnp.concatenate(parts, axis=1)

    def cross_copy(which, d, f):
        to = lax.rem(line + d, lines) * folds + lax.rem(side + f, folds)
        return remote(tile.at[which, to], across.at[which, d, f], cross_send.at[which, d, f],
                      cross_recv.at[which, d, f],
                      ((line * folds + lax.rem(side + f, folds)) * group + seat, mine))

    def tile_copy(which, d):
        to = lax.rem(line + d, lines)
        return remote(merged.at[which, d], got.at[which, d], tile_send.at[which, d], tile_recv.at[which, d],
                      ((to * folds + side) * group + seat, mine))

    def tiles_out(which):
        if which == 0:
            for part in range(2):
                for place in places:
                    basis_wait(part, *place)
        for e in range(1, group):
            for copy in held_copies(which, e, lax.rem(seat + group - e, group)):
                copy.wait_recv()
        fields = [field(which, i) for i in range(group)]
        for band in range(nb):
            value = dot(fields[0], full[0, band])
            for i in range(1, group):
                value = value + dot(fields[i], full[i, band])
            for t in range(per_seat):
                part = pack(value[:, t * rows : (t + 1) * rows])
                summed[which, band * per_seat + t] = part
                tile[which, band * per_seat + t] = part.astype(bf16)

        def emit(i, carry):
            for f in range(1, folds):
                cross_copy(which, lax.rem(i, lines), f).start()
            return carry

        lax.fori_loop(1, lines + 1, emit, 0, unroll=lines <= 4)

    def merge(which, d):
        acc = summed[which, lax.rem(line + d, lines) * folds + side]
        for f in range(1, folds):
            cross_copy(which, d, f).wait_recv()
            acc = acc + across[which, d, f].astype(f32)
        return acc

    def tiles_on(which):
        def emit(d, carry):
            merged[which, d] = merge(which, d).astype(bf16)
            tile_copy(which, d).start()
            return carry

        lax.fori_loop(1, lines, emit, 0, unroll=lines <= 4)

    def tiles_in(which):
        def collect(d, acc):
            tile_copy(which, d).wait_recv()
            return acc + got[which, d].astype(f32)

        return unpack(lax.fori_loop(1, lines, collect, merge(which, 0), unroll=lines <= 4))

    sigmas = sigma_values()
    previous = current = jnp.concatenate([raised[:, :columns], intro[:, :columns]], axis=0)
    for step in range(3):
        scaled = (mass * current.astype(f32)).astype(bf16)
        leaving = dot(stack[:sent, :], scaled)
        out[step] = leaving.astype(bf16)
        copies = []
        for index, (d, row, pieces) in enumerate(plan):
            span = pl.ds(row, slots * len(pieces))
            copies.append(
                remote(out.at[step, span], landed.at[step, span], halo_send.at[step, index],
                       halo_recv.at[step, index], partition(d))
            )
        launch(copies)
        local = dot(stack[sent:, :], scaled)
        if step == 0:
            scale_now, mixing = sigmas[0] / filter_half, 0.0
        else:
            scale_now, mixing = 2.0 * sigmas[step] / filter_half, sigmas[step - 1] * sigmas[step]
        after_send(step + 1)
        base = -(filter_centre * scale_now) * current.astype(f32)
        if step > 0:
            base = base - mixing * previous.astype(f32)
        if step == 2:
            ends = {}
            for _, _, pieces in plan:
                for row, kind, k, _ in pieces:
                    if kind == "back":
                        ends[k] = leaving[row : row + slots]
            outer = jnp.concatenate([ends[k] for k in range(width)], axis=0)
            share_field(
                0,
                scale_now * mass_own * local[ghosts:] + base[:owned],
                scale_now * mass_ghost * outer,
            )
            tiles_out(0)
        for copy in copies:
            copy.wait_recv()
        arrived = landed[step].astype(f32)
        ghost_sums = [local[k * slots : (k + 1) * slots] for k in range(width)]
        backs = [None] * width
        for _, _, pieces in plan:
            for row, kind, k, j in pieces:
                value = arrived[row : row + slots]
                if kind == "own":
                    ghost_sums[(k + reach) % width] += value
                elif kind == "back":
                    backs[(k + reach) % width] = landed[step, row : row + slots]
                else:
                    ghost_sums[(j + reach) % width] += value
        inner = local[ghosts:] + dot(send_hot_t, jnp.concatenate(backs, axis=0))
        sums = jnp.concatenate([inner] + ghost_sums, axis=0)
        previous, current = current, (scale_now * (mass * sums) + base).astype(bf16)

    scaled = (mass * current.astype(f32)).astype(bf16)
    image = mass * dot(stiff[...], scaled)
    share_field(1, image[:owned], image[owned:])
    f_ref[...] = current[:owned].astype(f32).T.astype(bf16)
    tiles_on(0)
    tiles_out(1)
    tiles_on(1)
    inter_ref[...] = tiles_in(0)
    ham_ref[...] = tiles_in(1)

    for copy in started:
        copy.wait_send()
    for which in range(2):
        def drain(d, carry):
            tile_copy(which, d).wait_send()
            return carry

        lax.fori_loop(1, lines, drain, 0)

        def drain_cross(d, carry):
            for f in range(1, folds):
                cross_copy(which, d, f).wait_send()
            return carry

        lax.fori_loop(0, lines, drain_cross, 0)


def deliver(*refs):
    for source, target in zip(refs[:3], refs[3:]):
        target[...] = source[...]


def on_device(n, nb, band_block, band_basis, mass_scale, cell_matrices, cell_nodes, cell_count, send_index):
    columns, owned = band_block.shape
    cell_slots, corners = cell_nodes.shape
    width, slots = send_index.shape[1:]
    cols = band_basis.shape[1]
    rows = cols * nb // n
    count = cell_slots * corners
    ghosts = width * slots
    total = owned + ghosts
    group = math.gcd(2, n // nb)
    teams = n // group
    folds = math.gcd(2, teams)
    lines = teams // folds
    per_seat = n // nb // group
    wide = -(-(columns + 3 + width) // 128) * 128
    packed = rows % 128 == 64 and columns % 32 == 0
    folded = ghosts == 64 and columns % 32 == 0
    tile_shape = (columns * rows // 128, 128) if packed else (columns, rows)
    edge_shape = (columns // 2, 128) if folded else (columns, ghosts)
    sent = routes(width // 2, slots)[1]
    vmem = pl.BlockSpec(memory_space=pltpu.VMEM)
    smem = pl.BlockSpec(memory_space=pltpu.SMEM)
    semaphores = pltpu.SemaphoreType.DMA
    filtered, inter, ham = pl.pallas_call(
        functools.partial(kernel, n, nb, group, packed, folded),
        out_shape=(
            jax.ShapeDtypeStruct((columns, owned), bf16),
            jax.ShapeDtypeStruct((columns, rows), f32),
            jax.ShapeDtypeStruct((columns, rows), f32),
        ),
        in_specs=[vmem, pl.BlockSpec(memory_space=pl.ANY), vmem, vmem, vmem, smem, vmem],
        out_specs=(vmem, vmem, vmem),
        scratch_shapes=[
            pltpu.VMEM((group, nb, total, per_seat * rows), bf16),
            pltpu.VMEM((owned, cols), bf16),
            pltpu.VMEM((group, owned, per_seat * rows), bf16),
            pltpu.VMEM((group, ghosts, per_seat * rows), bf16),
            pltpu.VMEM((group, ghosts, per_seat * rows), bf16),
            pltpu.VMEM((count, corners), bf16),
            pltpu.VMEM((total, count), bf16),
            pltpu.VMEM((total, count), bf16),
            pltpu.VMEM((total, total), bf16),
            pltpu.VMEM((sent + total, total), bf16),
            pltpu.VMEM((ghosts, wide), bf16),
            pltpu.VMEM((ghosts, wide), bf16),
            pltpu.VMEM((3, sent, columns), bf16),
            pltpu.VMEM((3, sent, columns), bf16),
            pltpu.VMEM((2, group, columns, owned), bf16),
            pltpu.VMEM((2, group) + edge_shape, bf16),
            pltpu.VMEM((2, teams) + tile_shape, f32),
            pltpu.VMEM((2, teams) + tile_shape, bf16),
            pltpu.VMEM((2, lines, folds) + tile_shape, bf16),
            pltpu.VMEM((2, lines) + tile_shape, bf16),
            pltpu.VMEM((2, lines) + tile_shape, bf16),
            semaphores,
            semaphores((width,)),
            semaphores((width,)),
            semaphores((3, 2 * width)),
            semaphores((3, 2 * width)),
            semaphores((width,)),
            semaphores((width,)),
            semaphores((2, group, nb)),
            semaphores((2, group, nb)),
            semaphores((2, group)),
            semaphores((2, group)),
            semaphores((2, group)),
            semaphores((2, group)),
            semaphores((2, lines, folds)),
            semaphores((2, lines, folds)),
            semaphores((2, lines)),
            semaphores((2, lines)),
        ],
        compiler_params=pltpu.CompilerParams(collective_id=0, has_side_effects=True, vmem_limit_bytes=60 << 20),
    )(
        band_block,
        band_basis,
        mass_scale.reshape(1, owned),
        cell_matrices,
        cell_nodes,
        cell_count,
        send_index,
    )
    anywhere = pl.BlockSpec(memory_space=pltpu.VMEM)
    filtered, inter, ham = pl.pallas_call(
        deliver,
        out_shape=tuple(jax.ShapeDtypeStruct(v.shape, v.dtype) for v in (filtered, inter, ham)),
        in_specs=[anywhere] * 3,
        out_specs=(anywhere,) * 3,
    )(filtered, inter, ham)
    return filtered, inter.T, ham.T


def solution(mesh):
    placed = (
        P("band", "mesh"),
        P("mesh", "band"),
        P("mesh"),
        P("mesh", None),
        P("mesh", None),
        P("mesh"),
        P("mesh", None, None),
    )
    return jax.shard_map(
        functools.partial(on_device, mesh.shape["mesh"], mesh.shape["band"]),
        mesh=mesh,
        in_specs=placed,
        out_specs=(P("band", "mesh"), P("mesh", "band"), P("mesh", "band")),
        check_vma=False,
    )
```

```python
import functools
import math
import jax
import jax.numpy as jnp
from jax import lax
from jax.experimental import pallas as pl
from jax.experimental.pallas import tpu as pltpu
from jax.sharding import PartitionSpec as P

filter_centre = 1.5
filter_half = 2.5
first_sigma = -0.625
MESH = pl.DeviceIdType.MESH
bf16 = jnp.bfloat16
f32 = jnp.float32


def sigma_values():
    values = [first_sigma]
    for _ in range(2):
        values.append(1.0 / (2.0 / first_sigma - values[-1]))
    return values


def neighbour_offset(neighbour, reach):
    if neighbour < reach:
        return neighbour + 1
    return reach - 1 - neighbour


def dot(a, b):
    return jnp.dot(a, b, preferred_element_type=f32)


def dot_nt(a, b):
    return lax.dot_general(a, b, (((1,), (1,)), ((), ())), preferred_element_type=f32)


def routes(reach, slots):
    width = 2 * reach
    offs = [neighbour_offset(k, reach) for k in range(width)]
    found, row = [], 0
    for d in [*range(1, width + 1), *range(-1, -width - 1, -1)]:
        pieces = []
        for k in range(width):
            if offs[k] == d:
                pieces += [("own", k, 0), ("back", k, 0)]
            pieces += [("third", k, j) for j in range(width) if offs[k] + offs[j] == d]
        found.append((d, row, [(row + slots * i, *piece) for i, piece in enumerate(pieces)]))
        row += slots * len(pieces)
    return found, row


def kernel(
    n, nb, group, packed, folded, x_ref, basis_ref, mass_ref, mats_ref, nodes_ref, count_ref, send_ref,
    f_ref, inter_ref, ham_ref,
    full, block, perm, ghost_out, ghost_in, mats, hots, coupled, stiff, stack, intro_out, intro, out, landed,
    held, edge, summed, tile, across, merged, kept, got,
    block_sem, intro_send, intro_recv, halo_send, halo_recv, gb_send, gb_recv, basis_send, basis_recv,
    held_send, held_recv, edge_send, edge_recv,
    cross_send, cross_recv, tile_send, tile_recv,
):
    me = lax.axis_index("mesh")
    mine = lax.axis_index("band")
    seat = lax.rem(me, group)
    team = me // group
    teams = n // group
    folds = math.gcd(2, n // nb // group)
    lines = teams // folds
    line, side = team // folds, lax.rem(team, folds)
    columns, owned = x_ref.shape
    width, slots = send_ref.shape[1:]
    reach = width // 2
    rows = inter_ref.shape[1]
    per_band = n // nb
    per_seat = per_band // group
    per_line = per_seat // folds
    ghosts = width * slots
    total = owned + ghosts
    cells, corners = nodes_ref.shape
    wide = intro.shape[1]
    plan, sent = routes(reach, slots)

    barrier = pltpu.get_barrier_semaphore()

    def greet(d, carry):
        pl.semaphore_signal(
            barrier, inc=1, device_id=(lax.rem(me + d, n), mine), device_id_type=MESH
        )
        return carry

    lax.fori_loop(1, n, greet, 0)
    for d in range(1, nb):
        for e in range(group):
            pl.semaphore_signal(
                barrier,
                inc=1,
                device_id=(team * group + lax.rem(seat + e, group), lax.rem(mine + d, nb)),
                device_id_type=MESH,
            )

    load = pltpu.make_async_copy(basis_ref, block, block_sem)
    load.start()

    def remote(source, target, send, recv, device):
        return pltpu.make_async_remote_copy(
            src_ref=source, dst_ref=target, send_sem=send, recv_sem=recv,
            device_id=device, device_id_type=MESH,
        )

    def partition(d):
        return (lax.rem(me + d + n, n), mine)

    def beside(e, d):
        return (team * group + lax.rem(seat + e, group), lax.rem(mine + d, nb))

    parts = (pl.ds(0, owned), pl.ds(owned, ghosts))
    ready = (perm, ghost_in)

    def basis_copy(part, e, d, q):
        source = ready[part].at[lax.rem(seat + e, group), q]
        target = full.at[seat, mine, q, parts[part]]
        if e == 0 and d == 0:
            return pltpu.make_async_copy(source, target, basis_recv.at[part, e, d, q])
        return remote(source, target, basis_send.at[part, e, d, q], basis_recv.at[part, e, d, q], beside(e, d))

    def basis_wait(d, q):
        for part in range(2):
            for e in range(group):
                if e == 0 and d == 0:
                    basis_copy(part, e, d, q).wait()
                    continue
                target = full.at[lax.rem(seat + group - e, group), lax.rem(mine + nb - d, nb), q, parts[part]]
                remote(ready[part].at[0, q], target, basis_send.at[part, e, d, q],
                       basis_recv.at[part, e, d, q], beside(e, d)).wait_recv()

    def basis_out(part, bands, q):
        for d in bands:
            for e in range(group):
                if e == 0 and d == 0:
                    basis_copy(part, e, d, q).start()
                else:
                    launch([basis_copy(part, e, d, q)])

    owned_ids = lax.broadcasted_iota(jnp.int32, (owned, slots), 0)
    hot_parts = [
        jnp.where(owned_ids == send_ref[0, k : k + 1, :], 1.0, 0.0) for k in range(width)
    ]
    send_hot_f = jnp.concatenate(hot_parts, axis=1)
    send_hot_t = send_hot_f.astype(bf16)
    send_hot = send_hot_f.T.astype(bf16)

    mass_row = mass_ref[...]
    high = mass_row.astype(bf16).astype(f32)
    middle = (mass_row - high).astype(bf16).astype(f32)
    low = mass_row - high - middle
    level = lax.broadcasted_iota(jnp.int32, (8, owned), 0)
    extra = jnp.where(level == 0, high, jnp.where(level == 1, middle, jnp.where(level == 2, low, 0.0)))
    raised = jnp.concatenate(
        [x_ref[...].astype(f32), extra, jnp.zeros((wide - columns - 8, owned), f32)], axis=0
    ).T.astype(bf16)
    first_id = columns + 3
    lane = lax.broadcasted_iota(jnp.int32, (ghosts, wide), 1)
    message = dot(send_hot, raised)
    numbers = dot(
        send_hot, (lax.broadcasted_iota(jnp.int32, (owned, wide), 0) + 1).astype(f32).astype(bf16)
    )
    for j in range(width):
        tiled = jnp.concatenate([numbers[j * slots : (j + 1) * slots]] * width, axis=0)
        message = jnp.where(lane == first_id + j, tiled, message)
    intro_out[...] = message.astype(bf16)
    mass_own = jnp.broadcast_to(mass_row, (8, owned)).T[:, :1]

    load.wait()
    for s in range(group):
        for q in range(per_line):
            starts = [(s + group * (q * folds + t)) * rows for t in range(folds)]
            perm[s, q] = jnp.concatenate([block[:, a : a + rows] for a in starts], axis=1)
            ghost_out[s, q] = dot(send_hot, perm[s, q]).astype(bf16)

    pl.semaphore_wait(barrier, n - 1 + (nb - 1) * group)

    def halo(source, target, send, recv, cut):
        return [
            remote(cut(source, k), cut(target, (k + reach) % width), send.at[k], recv.at[(k + reach) % width],
                   partition(neighbour_offset(k, reach)))
            for k in range(width)
        ]

    started = []

    def launch(copies):
        for copy in copies:
            copy.start()
        started.extend(copies)

    intros = halo(intro_out, intro, intro_send, intro_recv, lambda ref, k: ref.at[pl.ds(k * slots, slots)])
    launch(intros)
    rims = halo(ghost_out, ghost_in, gb_send, gb_recv, lambda ref, k: ref.at[:, :, pl.ds(k * slots, slots)])
    launch(rims)
    def after_send(index):
        far = range(1, nb)
        if index == 0:
            basis_out(0, far, 0)
            for q in range(per_line):
                basis_out(0, range(1), q)
        if index == 1:
            for copy in rims:
                copy.wait_recv()
            basis_out(1, far, 0)
            for q in range(1, per_line):
                basis_out(0, far, q)
                basis_out(1, far, q)
            for q in range(per_line):
                basis_out(1, range(1), q)

    after_send(0)

    fold = 128 // corners
    strips = corners // fold
    stacked = jnp.concatenate([mats_ref[:, a * 128 : (a + 1) * 128] for a in range(strips)], axis=0)
    row = lax.broadcasted_iota(jnp.int32, (cells * corners, cells * strips), 0)
    column = lax.broadcasted_iota(jnp.int32, (cells * corners, cells * strips), 1)
    picked = (row % corners) // fold * cells + row // corners == column
    spread = dot(jnp.where(picked, 1.0, 0.0).astype(bf16), stacked)
    turn = lax.broadcasted_iota(jnp.int32, (cells * corners, corners), 0) % fold
    unfolded = spread[:, :corners]
    for a in range(1, fold):
        unfolded = jnp.where(turn == a, spread[:, a * corners : (a + 1) * corners], unfolded)
    mats[...] = unfolded.astype(bf16)

    live = count_ref[0]
    total_ids = lax.broadcasted_iota(jnp.int32, (total, corners), 0)
    for c in range(cells):
        hot = jnp.where(
            jnp.logical_and(total_ids == nodes_ref[c : c + 1, :], c < live), 1.0, 0.0
        ).astype(bf16)
        part = slice(c * corners, (c + 1) * corners)
        hots[:, part] = hot
        coupled[:, part] = dot_nt(hot, mats[part, :]).astype(bf16)
    stiff[...] = dot_nt(hots[...], coupled[...]).astype(bf16)

    own_rows = dot(send_hot, stiff[:owned, :]).astype(bf16)
    for _, _, pieces in plan:
        for row, kind, k, _ in pieces:
            if kind == "own":
                stack[row : row + slots, :] = own_rows[k * slots : (k + 1) * slots]
            if kind == "back":
                stack[row : row + slots, :] = stiff[owned + k * slots : owned + (k + 1) * slots, :]
    stack[sent + ghosts :, :] = stiff[:owned, :]

    for copy in intros:
        copy.wait_recv()
    there = intro[...].astype(f32)
    turned = there.T
    mass_ghost = there[:, columns : columns + 1] + there[:, columns + 1 : columns + 2] + there[:, columns + 2 : columns + 3]
    mass = jnp.concatenate([mass_own, mass_ghost], axis=0)
    slot_lane = lax.broadcasted_iota(jnp.int32, (1, ghosts), 1)
    listed = jnp.zeros((1, ghosts), f32)
    for k in range(width):
        at = first_id + (k + reach) % width
        inside = jnp.logical_and(slot_lane >= k * slots, slot_lane < (k + 1) * slots)
        listed = jnp.where(inside, turned[at : at + 1, :], listed)
    piece_lane = lax.broadcasted_iota(jnp.int32, (slots, ghosts), 1)
    mixers = []
    for k in range(width):
        inside = jnp.logical_and(piece_lane >= k * slots, piece_lane < (k + 1) * slots)
        for j in range(width):
            column = there[k * slots : (k + 1) * slots, first_id + j : first_id + j + 1]
            mixers.append(jnp.where(jnp.logical_and(inside, column == listed), 1.0, 0.0))
    mixed = dot(jnp.concatenate(mixers, axis=0).astype(bf16), stiff[owned:, :]).astype(bf16)

    def mixed_rows(k, j):
        return mixed[(k * width + j) * slots : (k * width + j + 1) * slots]

    for _, _, pieces in plan:
        for row, kind, k, j in pieces:
            if kind == "third":
                stack[row : row + slots, :] = mixed_rows(k, j)
    for k in range(width):
        stack[sent + k * slots : sent + (k + 1) * slots, :] = mixed_rows(k, (k + reach) % width)

    def held_copies(which, e, owner):
        return [
            remote(ref.at[which, owner], ref.at[which, owner], send.at[which, e], recv.at[which, e], beside(e, 0))
            for ref, send, recv in ((held, held_send, held_recv), (edge, edge_send, edge_recv))
        ]

    def share_field(which, inner, outer):
        held[which, seat] = inner.T.astype(bf16)
        outer = outer.T
        if folded:
            outer = jnp.concatenate([outer[: columns // 2], outer[columns // 2 :]], axis=1)
        edge[which, seat] = outer.astype(bf16)
        for e in range(1, group):
            launch(held_copies(which, e, seat))

    def field(which, i):
        outer = edge[which, i]
        if folded:
            outer = jnp.concatenate([outer[:, :ghosts], outer[:, ghosts:]], axis=0)
        return jnp.concatenate([held[which, i], outer], axis=1)

    def pack(value):
        if not packed:
            return value
        half = columns // 2
        left = rows - rows % 128
        rest = jnp.concatenate([value[:half, left:], value[half:, left:]], axis=1)
        parts = [value[:, a : a + 128] for a in range(0, left, 128)]
        return jnp.concatenate(parts + [rest], axis=0)

    def unpack(value):
        if not packed:
            return value
        full_parts = rows // 128
        parts = [value[a * columns : (a + 1) * columns] for a in range(full_parts)]
        rest = value[full_parts * columns :]
        parts.append(jnp.concatenate([rest[:, :64], rest[:, 64:]], axis=0))
        return jnp.concatenate(parts, axis=1)

    chunks = [(d, q) for q in range(per_line) for d in range(nb)]
    chunks.sort(key=lambda chunk: chunk[0] > 0)
    late = [chunk for chunk in chunks if chunk[0] > 0 and chunk[1] == per_line - 1]
    early = [chunk for chunk in chunks if chunk not in late]

    def target_line(d, q):
        return lax.rem(mine + nb - d, nb) * per_line + q

    def cross_copy(which, d, q, f):
        to = target_line(d, q)
        there = lax.rem(side + f, folds)
        return remote(tile.at[which, to, there], across.at[which, to, f], cross_send.at[which, to, f],
                      cross_recv.at[which, to, f], ((line * folds + there) * group + seat, mine))

    def tile_copy(which, to):
        return remote(merged.at[which, to], got.at[which, line], tile_send.at[which, to],
                      tile_recv.at[which, line], ((to * folds + side) * group + seat, mine))

    def fields_in(which):
        for e in range(1, group):
            for copy in held_copies(which, e, lax.rem(seat + group - e, group)):
                copy.wait_recv()

    def multiply(which, some):
        fields = [field(which, i) for i in range(group)]
        for d, q in some:
            band, to = lax.rem(mine + nb - d, nb), target_line(d, q)
            value = dot(fields[0], full[0, band, q])
            for i in range(1, group):
                value = value + dot(fields[i], full[i, band, q])
            for t in range(folds):
                part = pack(value[:, t * rows : (t + 1) * rows])
                summed[which, to, t] = part
                tile[which, to, t] = part.astype(bf16)
            launch([cross_copy(which, d, q, f) for f in range(1, folds)])

    def tiles_on(which, some):
        for d, q in some:
            to = target_line(d, q)
            acc = summed[which, to, side]
            for f in range(1, folds):
                cross_copy(which, d, q, f).wait_recv()
                acc = acc + across[which, to, f].astype(f32)
            merged[which, to] = acc.astype(bf16)

            @pl.when(to != line)
            def _():
                tile_copy(which, to).start()

            @pl.when(to == line)
            def _():
                kept[which] = acc

    def tiles_in(which):
        def collect(d, acc):
            source = lax.rem(line + d, lines)
            remote(merged.at[which, source], got.at[which, source], tile_send.at[which, source],
                   tile_recv.at[which, source], ((source * folds + side) * group + seat, mine)).wait_recv()
            return acc + got[which, source].astype(f32)

        return unpack(lax.fori_loop(1, lines, collect, kept[which], unroll=lines <= 4))

    sigmas = sigma_values()
    previous = current = jnp.concatenate([raised[:, :columns], intro[:, :columns]], axis=0)
    for step in range(3):
        scaled = (mass * current.astype(f32)).astype(bf16)
        leaving = dot(stack[:sent, :], scaled)
        out[step] = leaving.astype(bf16)
        copies = []
        for index, (d, row, pieces) in enumerate(plan):
            span = pl.ds(row, slots * len(pieces))
            copies.append(
                remote(out.at[step, span], landed.at[step, span], halo_send.at[step, index],
                       halo_recv.at[step, index], partition(d))
            )
        launch(copies)
        local = dot(stack[sent:, :], scaled)
        if step == 0:
            scale_now, mixing = sigmas[0] / filter_half, 0.0
        else:
            scale_now, mixing = 2.0 * sigmas[step] / filter_half, sigmas[step - 1] * sigmas[step]
        after_send(step + 1)
        base = -(filter_centre * scale_now) * current.astype(f32)
        if step > 0:
            base = base - mixing * previous.astype(f32)
        if step == 2:
            ends = {}
            for _, _, pieces in plan:
                for row, kind, k, _ in pieces:
                    if kind == "back":
                        ends[k] = leaving[row : row + slots]
            outer = jnp.concatenate([ends[k] for k in range(width)], axis=0)
            share_field(
                0,
                scale_now * mass_own * local[ghosts:] + base[:owned],
                scale_now * mass_ghost * outer,
            )
            fields_in(0)
            for chunk in early:
                basis_wait(*chunk)
                multiply(0, [chunk])
        for copy in copies:
            copy.wait_recv()
        arrived = landed[step].astype(f32)
        ghost_sums = [local[k * slots : (k + 1) * slots] for k in range(width)]
        backs = [None] * width
        for _, _, pieces in plan:
            for row, kind, k, j in pieces:
                value = arrived[row : row + slots]
                if kind == "own":
                    ghost_sums[(k + reach) % width] += value
                elif kind == "back":
                    backs[(k + reach) % width] = landed[step, row : row + slots]
                else:
                    ghost_sums[(j + reach) % width] += value
        inner = local[ghosts:] + dot(send_hot_t, jnp.concatenate(backs, axis=0))
        sums = jnp.concatenate([inner] + ghost_sums, axis=0)
        previous, current = current, (scale_now * (mass * sums) + base).astype(bf16)

    scaled = (mass * current.astype(f32)).astype(bf16)
    image = mass * dot(stiff[...], scaled)
    share_field(1, image[:owned], image[owned:])
    f_ref[...] = current[:owned].astype(f32).T.astype(bf16)
    fields_in(1)
    multiply(1, early)
    tiles_on(0, early)
    for chunk in late:
        basis_wait(*chunk)
    multiply(1, late)
    multiply(0, late)
    tiles_on(1, early)
    tiles_on(1, late)
    tiles_on(0, late)
    inter_ref[...] = tiles_in(0)
    ham_ref[...] = tiles_in(1)

    for copy in started:
        copy.wait_send()
    for which in range(2):
        def drain(d, carry):
            tile_copy(which, lax.rem(line + d, lines)).wait_send()
            return carry

        lax.fori_loop(1, lines, drain, 0)


def deliver(*refs):
    for source, target in zip(refs[:3], refs[3:]):
        target[...] = source[...]


def on_device(n, nb, band_block, band_basis, mass_scale, cell_matrices, cell_nodes, cell_count, send_index):
    columns, owned = band_block.shape
    cell_slots, corners = cell_nodes.shape
    width, slots = send_index.shape[1:]
    cols = band_basis.shape[1]
    rows = cols * nb // n
    count = cell_slots * corners
    ghosts = width * slots
    total = owned + ghosts
    group = math.gcd(2, n // nb)
    teams = n // group
    per_seat = n // nb // group
    folds = math.gcd(2, per_seat)
    lines = teams // folds
    per_line = per_seat // folds
    wide = -(-(columns + 3 + width) // 128) * 128
    packed = rows % 128 == 64 and columns % 32 == 0
    folded = ghosts == 64 and columns % 32 == 0
    tile_shape = (columns * rows // 128, 128) if packed else (columns, rows)
    edge_shape = (columns // 2, 128) if folded else (columns, ghosts)
    sent = routes(width // 2, slots)[1]
    vmem = pl.BlockSpec(memory_space=pltpu.VMEM)
    smem = pl.BlockSpec(memory_space=pltpu.SMEM)
    semaphores = pltpu.SemaphoreType.DMA
    filtered, inter, ham = pl.pallas_call(
        functools.partial(kernel, n, nb, group, packed, folded),
        out_shape=(
            jax.ShapeDtypeStruct((columns, owned), bf16),
            jax.ShapeDtypeStruct((columns, rows), f32),
            jax.ShapeDtypeStruct((columns, rows), f32),
        ),
        in_specs=[vmem, pl.BlockSpec(memory_space=pl.ANY), vmem, vmem, vmem, smem, vmem],
        out_specs=(vmem, vmem, vmem),
        scratch_shapes=[
            pltpu.VMEM((group, nb, per_line, total, folds * rows), bf16),
            pltpu.VMEM((owned, cols), bf16),
            pltpu.VMEM((group, per_line, owned, folds * rows), bf16),
            pltpu.VMEM((group, per_line, ghosts, folds * rows), bf16),
            pltpu.VMEM((group, per_line, ghosts, folds * rows), bf16),
            pltpu.VMEM((count, corners), bf16),
            pltpu.VMEM((total, count), bf16),
            pltpu.VMEM((total, count), bf16),
            pltpu.VMEM((total, total), bf16),
            pltpu.VMEM((sent + total, total), bf16),
            pltpu.VMEM((ghosts, wide), bf16),
            pltpu.VMEM((ghosts, wide), bf16),
            pltpu.VMEM((3, sent, columns), bf16),
            pltpu.VMEM((3, sent, columns), bf16),
            pltpu.VMEM((2, group, columns, owned), bf16),
            pltpu.VMEM((2, group) + edge_shape, bf16),
            pltpu.VMEM((2, lines, folds) + tile_shape, f32),
            pltpu.VMEM((2, lines, folds) + tile_shape, bf16),
            pltpu.VMEM((2, lines, folds) + tile_shape, bf16),
            pltpu.VMEM((2, lines) + tile_shape, bf16),
            pltpu.VMEM((2,) + tile_shape, f32),
            pltpu.VMEM((2, lines) + tile_shape, bf16),
            semaphores,
            semaphores((width,)),
            semaphores((width,)),
            semaphores((3, 2 * width)),
            semaphores((3, 2 * width)),
            semaphores((width,)),
            semaphores((width,)),
            semaphores((2, group, nb, per_line)),
            semaphores((2, group, nb, per_line)),
            semaphores((2, group)),
            semaphores((2, group)),
            semaphores((2, group)),
            semaphores((2, group)),
            semaphores((2, lines, folds)),
            semaphores((2, lines, folds)),
            semaphores((2, lines)),
            semaphores((2, lines)),
        ],
        compiler_params=pltpu.CompilerParams(collective_id=0, has_side_effects=True, vmem_limit_bytes=60 << 20),
    )(
        band_block,
        band_basis,
        mass_scale.reshape(1, owned),
        cell_matrices,
        cell_nodes,
        cell_count,
        send_index,
    )
    anywhere = pl.BlockSpec(memory_space=pltpu.VMEM)
    filtered, inter, ham = pl.pallas_call(
        deliver,
        out_shape=tuple(jax.ShapeDtypeStruct(v.shape, v.dtype) for v in (filtered, inter, ham)),
        in_specs=[anywhere] * 3,
        out_specs=(anywhere,) * 3,
    )(filtered, inter, ham)
    return filtered, inter.T, ham.T


def solution(mesh):
    placed = (
        P("band", "mesh"),
        P("mesh", "band"),
        P("mesh"),
        P("mesh", None),
        P("mesh", None),
        P("mesh"),
        P("mesh", None, None),
    )
    return jax.shard_map(
        functools.partial(on_device, mesh.shape["mesh"], mesh.shape["band"]),
        mesh=mesh,
        in_specs=placed,
        out_specs=(P("band", "mesh"), P("mesh", "band"), P("mesh", "band")),
        check_vma=False,
    )
```

```python
import functools
import math
import jax
import jax.numpy as jnp
from jax import lax
from jax.experimental import pallas as pl
from jax.experimental.pallas import tpu as pltpu
from jax.sharding import PartitionSpec as P

filter_centre = 1.5
filter_half = 2.5
first_sigma = -0.625
MESH = pl.DeviceIdType.MESH
bf16 = jnp.bfloat16
f32 = jnp.float32


def sigma_values():
    values = [first_sigma]
    for _ in range(2):
        values.append(1.0 / (2.0 / first_sigma - values[-1]))
    return values


def neighbour_offset(neighbour, reach):
    if neighbour < reach:
        return neighbour + 1
    return reach - 1 - neighbour


def dot(a, b):
    return jnp.dot(a, b, preferred_element_type=f32)


def dot_nt(a, b):
    return lax.dot_general(a, b, (((1,), (1,)), ((), ())), preferred_element_type=f32)


def routes(reach, slots):
    width = 2 * reach
    offs = [neighbour_offset(k, reach) for k in range(width)]
    found, row = [], 0
    for d in [*range(1, width + 1), *range(-1, -width - 1, -1)]:
        pieces = []
        for k in range(width):
            if offs[k] == d:
                pieces += [("own", k, 0), ("back", k, 0)]
            pieces += [("third", k, j) for j in range(width) if offs[k] + offs[j] == d]
        found.append((d, row, [(row + slots * i, *piece) for i, piece in enumerate(pieces)]))
        row += slots * len(pieces)
    return found, row


def kernel(
    n, nb, group, packed, folded, x_hbm, basis_hbm, mass_hbm, mats_hbm, nodes_hbm, count_ref, send_hbm,
    f_ref, inter_ref, ham_ref,
    x_ref, block, mass_ref, mats_ref, nodes_ref, send_ref,
    full, perm, ghost_out, ghost_in, mats, hots, coupled, stiff, stack, intro_out, intro, out, landed,
    held, edge, summed, tile, across, merged, kept, got,
    load_sem, intro_send, intro_recv, halo_send, halo_recv, gb_send, gb_recv, basis_send, basis_recv,
    held_send, held_recv, edge_send, edge_recv,
    cross_send, cross_recv, tile_send, tile_recv,
):
    me = lax.axis_index("mesh")
    mine = lax.axis_index("band")
    seat = lax.rem(me, group)
    team = me // group
    teams = n // group
    folds = math.gcd(2, n // nb // group)
    lines = teams // folds
    line, side = team // folds, lax.rem(team, folds)
    columns, owned = x_ref.shape
    width, slots = send_ref.shape[1:]
    reach = width // 2
    rows = inter_ref.shape[1]
    per_band = n // nb
    per_seat = per_band // group
    per_line = per_seat // folds
    ghosts = width * slots
    total = owned + ghosts
    cells, corners = nodes_ref.shape
    wide = intro.shape[1]
    plan, sent = routes(reach, slots)

    barrier = pltpu.get_barrier_semaphore()

    def greet(d, carry):
        pl.semaphore_signal(
            barrier, inc=1, device_id=(lax.rem(me + d, n), mine), device_id_type=MESH
        )
        return carry

    lax.fori_loop(1, n, greet, 0)
    for d in range(1, nb):
        for e in range(group):
            pl.semaphore_signal(
                barrier,
                inc=1,
                device_id=(team * group + lax.rem(seat + e, group), lax.rem(mine + d, nb)),
                device_id_type=MESH,
            )

    loads = [
        pltpu.make_async_copy(source, target, load_sem.at[i])
        for i, (source, target) in enumerate((
            (send_hbm, send_ref), (mass_hbm, mass_ref), (x_hbm, x_ref), (basis_hbm, block),
            (mats_hbm, mats_ref), (nodes_hbm, nodes_ref),
        ))
    ]
    for load in loads:
        load.start()
    def remote(source, target, send, recv, device):
        return pltpu.make_async_remote_copy(
            src_ref=source, dst_ref=target, send_sem=send, recv_sem=recv,
            device_id=device, device_id_type=MESH,
        )

    def partition(d):
        return (lax.rem(me + d + n, n), mine)

    def beside(e, d):
        return (team * group + lax.rem(seat + e, group), lax.rem(mine + d, nb))

    parts = (pl.ds(0, owned), pl.ds(owned, ghosts))
    ready = (perm, ghost_in)

    def basis_copy(part, e, d, q):
        source = ready[part].at[lax.rem(seat + e, group), q]
        target = full.at[seat, mine, q, parts[part]]
        if e == 0 and d == 0:
            return pltpu.make_async_copy(source, target, basis_recv.at[part, e, d, q])
        return remote(source, target, basis_send.at[part, e, d, q], basis_recv.at[part, e, d, q], beside(e, d))

    def basis_wait(d, q):
        for part in range(2):
            for e in range(group):
                if e == 0 and d == 0:
                    basis_copy(part, e, d, q).wait()
                    continue
                target = full.at[lax.rem(seat + group - e, group), lax.rem(mine + nb - d, nb), q, parts[part]]
                remote(ready[part].at[0, q], target, basis_send.at[part, e, d, q],
                       basis_recv.at[part, e, d, q], beside(e, d)).wait_recv()

    def basis_out(part, bands, q):
        for d in bands:
            for e in range(group):
                if e == 0 and d == 0:
                    basis_copy(part, e, d, q).start()
                else:
                    launch([basis_copy(part, e, d, q)])

    for load in loads[:3]:
        load.wait()
    owned_ids = lax.broadcasted_iota(jnp.int32, (owned, slots), 0)
    hot_parts = [
        jnp.where(owned_ids == send_ref[0, k : k + 1, :], 1.0, 0.0) for k in range(width)
    ]
    send_hot_f = jnp.concatenate(hot_parts, axis=1)
    send_hot_t = send_hot_f.astype(bf16)
    send_hot = send_hot_f.T.astype(bf16)

    mass_row = mass_ref[...]
    high = mass_row.astype(bf16).astype(f32)
    middle = (mass_row - high).astype(bf16).astype(f32)
    low = mass_row - high - middle
    level = lax.broadcasted_iota(jnp.int32, (8, owned), 0)
    extra = jnp.where(level == 0, high, jnp.where(level == 1, middle, jnp.where(level == 2, low, 0.0)))
    raised = jnp.concatenate(
        [x_ref[...].astype(f32), extra, jnp.zeros((wide - columns - 8, owned), f32)], axis=0
    ).T.astype(bf16)
    first_id = columns + 3
    lane = lax.broadcasted_iota(jnp.int32, (ghosts, wide), 1)
    message = dot(send_hot, raised)
    numbers = dot(
        send_hot, (lax.broadcasted_iota(jnp.int32, (owned, wide), 0) + 1).astype(f32).astype(bf16)
    )
    for j in range(width):
        tiled = jnp.concatenate([numbers[j * slots : (j + 1) * slots]] * width, axis=0)
        message = jnp.where(lane == first_id + j, tiled, message)
    intro_out[...] = message.astype(bf16)
    mass_own = jnp.broadcast_to(mass_row, (8, owned)).T[:, :1]

    loads[3].wait()
    for s in range(group):
        for q in range(per_line):
            starts = [(s + group * (q * folds + t)) * rows for t in range(folds)]
            perm[s, q] = jnp.concatenate([block[:, a : a + rows] for a in starts], axis=1)
            ghost_out[s, q] = dot(send_hot, perm[s, q]).astype(bf16)

    pl.semaphore_wait(barrier, n - 1 + (nb - 1) * group)

    def halo(source, target, send, recv, cut):
        return [
            remote(cut(source, k), cut(target, (k + reach) % width), send.at[k], recv.at[(k + reach) % width],
                   partition(neighbour_offset(k, reach)))
            for k in range(width)
        ]

    started = []

    def launch(copies):
        for copy in copies:
            copy.start()
        started.extend(copies)

    intros = halo(intro_out, intro, intro_send, intro_recv, lambda ref, k: ref.at[pl.ds(k * slots, slots)])
    launch(intros)
    rims = halo(ghost_out, ghost_in, gb_send, gb_recv, lambda ref, k: ref.at[:, :, pl.ds(k * slots, slots)])
    launch(rims)
    def after_send(index):
        far = range(1, nb)
        if index == 0:
            basis_out(0, far, 0)
            for q in range(per_line):
                basis_out(0, range(1), q)
        if index == 1:
            for copy in rims:
                copy.wait_recv()
            basis_out(1, far, 0)
            for q in range(1, per_line):
                basis_out(0, far, q)
                basis_out(1, far, q)
            for q in range(per_line):
                basis_out(1, range(1), q)

    after_send(0)

    for load in loads[4:]:
        load.wait()
    fold = 128 // corners
    strips = corners // fold
    stacked = jnp.concatenate([mats_ref[:, a * 128 : (a + 1) * 128] for a in range(strips)], axis=0)
    row = lax.broadcasted_iota(jnp.int32, (cells * corners, cells * strips), 0)
    column = lax.broadcasted_iota(jnp.int32, (cells * corners, cells * strips), 1)
    picked = (row % corners) // fold * cells + row // corners == column
    spread = dot(jnp.where(picked, 1.0, 0.0).astype(bf16), stacked)
    turn = lax.broadcasted_iota(jnp.int32, (cells * corners, corners), 0) % fold
    unfolded = spread[:, :corners]
    for a in range(1, fold):
        unfolded = jnp.where(turn == a, spread[:, a * corners : (a + 1) * corners], unfolded)
    mats[...] = unfolded.astype(bf16)

    live = count_ref[0]
    total_ids = lax.broadcasted_iota(jnp.int32, (total, corners), 0)
    for c in range(cells):
        hot = jnp.where(
            jnp.logical_and(total_ids == nodes_ref[c : c + 1, :], c < live), 1.0, 0.0
        ).astype(bf16)
        part = slice(c * corners, (c + 1) * corners)
        hots[:, part] = hot
        coupled[:, part] = dot_nt(hot, mats[part, :]).astype(bf16)
    stiff[...] = dot_nt(hots[...], coupled[...]).astype(bf16)

    own_rows = dot(send_hot, stiff[:owned, :]).astype(bf16)
    for _, _, pieces in plan:
        for row, kind, k, _ in pieces:
            if kind == "own":
                stack[row : row + slots, :] = own_rows[k * slots : (k + 1) * slots]
            if kind == "back":
                stack[row : row + slots, :] = stiff[owned + k * slots : owned + (k + 1) * slots, :]
    stack[sent + ghosts :, :] = stiff[:owned, :]

    for copy in intros:
        copy.wait_recv()
    there = intro[...].astype(f32)
    turned = there.T
    mass_ghost = there[:, columns : columns + 1] + there[:, columns + 1 : columns + 2] + there[:, columns + 2 : columns + 3]
    mass = jnp.concatenate([mass_own, mass_ghost], axis=0)
    slot_lane = lax.broadcasted_iota(jnp.int32, (1, ghosts), 1)
    listed = jnp.zeros((1, ghosts), f32)
    for k in range(width):
        at = first_id + (k + reach) % width
        inside = jnp.logical_and(slot_lane >= k * slots, slot_lane < (k + 1) * slots)
        listed = jnp.where(inside, turned[at : at + 1, :], listed)
    piece_lane = lax.broadcasted_iota(jnp.int32, (slots, ghosts), 1)
    mixers = []
    for k in range(width):
        inside = jnp.logical_and(piece_lane >= k * slots, piece_lane < (k + 1) * slots)
        for j in range(width):
            column = there[k * slots : (k + 1) * slots, first_id + j : first_id + j + 1]
            mixers.append(jnp.where(jnp.logical_and(inside, column == listed), 1.0, 0.0))
    mixed = dot(jnp.concatenate(mixers, axis=0).astype(bf16), stiff[owned:, :]).astype(bf16)

    def mixed_rows(k, j):
        return mixed[(k * width + j) * slots : (k * width + j + 1) * slots]

    for _, _, pieces in plan:
        for row, kind, k, j in pieces:
            if kind == "third":
                stack[row : row + slots, :] = mixed_rows(k, j)
    for k in range(width):
        stack[sent + k * slots : sent + (k + 1) * slots, :] = mixed_rows(k, (k + reach) % width)

    def held_copies(which, e, owner):
        return [
            remote(ref.at[which, owner], ref.at[which, owner], send.at[which, e], recv.at[which, e], beside(e, 0))
            for ref, send, recv in ((held, held_send, held_recv), (edge, edge_send, edge_recv))
        ]

    def share_field(which, inner, outer):
        held[which, seat] = inner.T.astype(bf16)
        outer = outer.T
        if folded:
            outer = jnp.concatenate([outer[: columns // 2], outer[columns // 2 :]], axis=1)
        edge[which, seat] = outer.astype(bf16)
        for e in range(1, group):
            launch(held_copies(which, e, seat))

    def field(which, i):
        outer = edge[which, i]
        if folded:
            outer = jnp.concatenate([outer[:, :ghosts], outer[:, ghosts:]], axis=0)
        return jnp.concatenate([held[which, i], outer], axis=1)

    def pack(value):
        if not packed:
            return value
        half = columns // 2
        left = rows - rows % 128
        rest = jnp.concatenate([value[:half, left:], value[half:, left:]], axis=1)
        parts = [value[:, a : a + 128] for a in range(0, left, 128)]
        return jnp.concatenate(parts + [rest], axis=0)

    def unpack(value):
        if not packed:
            return value
        full_parts = rows // 128
        parts = [value[a * columns : (a + 1) * columns] for a in range(full_parts)]
        rest = value[full_parts * columns :]
        parts.append(jnp.concatenate([rest[:, :64], rest[:, 64:]], axis=0))
        return jnp.concatenate(parts, axis=1)

    chunks = [(d, q) for q in range(per_line) for d in range(nb)]
    chunks.sort(key=lambda chunk: chunk[0] > 0)
    late = [chunk for chunk in chunks if chunk[0] > 0 and chunk[1] == per_line - 1]
    early = [chunk for chunk in chunks if chunk not in late]

    def target_line(d, q):
        return lax.rem(mine + nb - d, nb) * per_line + q

    def cross_copy(which, d, q, f):
        to = target_line(d, q)
        there = lax.rem(side + f, folds)
        return remote(tile.at[which, to, there], across.at[which, to, f], cross_send.at[which, to, f],
                      cross_recv.at[which, to, f], ((line * folds + there) * group + seat, mine))

    def tile_copy(which, to):
        return remote(merged.at[which, to], got.at[which, line], tile_send.at[which, to],
                      tile_recv.at[which, line], ((to * folds + side) * group + seat, mine))

    def fields_in(which):
        for e in range(1, group):
            for copy in held_copies(which, e, lax.rem(seat + group - e, group)):
                copy.wait_recv()

    def multiply(which, some):
        fields = [field(which, i) for i in range(group)]
        for d, q in some:
            band, to = lax.rem(mine + nb - d, nb), target_line(d, q)
            value = dot(fields[0], full[0, band, q])
            for i in range(1, group):
                value = value + dot(fields[i], full[i, band, q])
            for t in range(folds):
                part = pack(value[:, t * rows : (t + 1) * rows])
                summed[which, to, t] = part
                tile[which, to, t] = part.astype(bf16)
            launch([cross_copy(which, d, q, f) for f in range(1, folds)])

    def tiles_on(which, some):
        for d, q in some:
            to = target_line(d, q)
            acc = summed[which, to, side]
            for f in range(1, folds):
                cross_copy(which, d, q, f).wait_recv()
                acc = acc + across[which, to, f].astype(f32)
            merged[which, to] = acc.astype(bf16)

            @pl.when(to != line)
            def _():
                tile_copy(which, to).start()

            @pl.when(to == line)
            def _():
                kept[which] = acc

    def tiles_in(which):
        def collect(d, acc):
            source = lax.rem(line + d, lines)
            remote(merged.at[which, source], got.at[which, source], tile_send.at[which, source],
                   tile_recv.at[which, source], ((source * folds + side) * group + seat, mine)).wait_recv()
            return acc + got[which, source].astype(f32)

        return unpack(lax.fori_loop(1, lines, collect, kept[which], unroll=lines <= 4))

    sigmas = sigma_values()
    previous = current = jnp.concatenate([raised[:, :columns], intro[:, :columns]], axis=0)
    for step in range(3):
        scaled = (mass * current.astype(f32)).astype(bf16)
        leaving = dot(stack[:sent, :], scaled)
        out[step] = leaving.astype(bf16)
        copies = []
        for index, (d, row, pieces) in enumerate(plan):
            span = pl.ds(row, slots * len(pieces))
            copies.append(
                remote(out.at[step, span], landed.at[step, span], halo_send.at[step, index],
                       halo_recv.at[step, index], partition(d))
            )
        launch(copies)
        local = dot(stack[sent:, :], scaled)
        if step == 0:
            scale_now, mixing = sigmas[0] / filter_half, 0.0
        else:
            scale_now, mixing = 2.0 * sigmas[step] / filter_half, sigmas[step - 1] * sigmas[step]
        after_send(step + 1)
        base = -(filter_centre * scale_now) * current.astype(f32)
        if step > 0:
            base = base - mixing * previous.astype(f32)
        if step == 2:
            ends = {}
            for _, _, pieces in plan:
                for row, kind, k, _ in pieces:
                    if kind == "back":
                        ends[k] = leaving[row : row + slots]
            outer = jnp.concatenate([ends[k] for k in range(width)], axis=0)
            share_field(
                0,
                scale_now * mass_own * local[ghosts:] + base[:owned],
                scale_now * mass_ghost * outer,
            )
            fields_in(0)
            for chunk in early:
                basis_wait(*chunk)
                multiply(0, [chunk])
        for copy in copies:
            copy.wait_recv()
        arrived = landed[step].astype(f32)
        ghost_sums = [local[k * slots : (k + 1) * slots] for k in range(width)]
        backs = [None] * width
        for _, _, pieces in plan:
            for row, kind, k, j in pieces:
                value = arrived[row : row + slots]
                if kind == "own":
                    ghost_sums[(k + reach) % width] += value
                elif kind == "back":
                    backs[(k + reach) % width] = landed[step, row : row + slots]
                else:
                    ghost_sums[(j + reach) % width] += value
        inner = local[ghosts:] + dot(send_hot_t, jnp.concatenate(backs, axis=0))
        sums = jnp.concatenate([inner] + ghost_sums, axis=0)
        previous, current = current, (scale_now * (mass * sums) + base).astype(bf16)

    scaled = (mass * current.astype(f32)).astype(bf16)
    image = mass * dot(stiff[...], scaled)
    share_field(1, image[:owned], image[owned:])
    f_ref[...] = current[:owned].astype(f32).T.astype(bf16)
    fields_in(1)
    multiply(1, early)
    tiles_on(0, early)
    for chunk in late:
        basis_wait(*chunk)
    multiply(1, late)
    multiply(0, late)
    tiles_on(1, early)
    tiles_on(1, late)
    tiles_on(0, late)
    inter_ref[...] = tiles_in(0)
    ham_ref[...] = tiles_in(1)

    for copy in started:
        copy.wait_send()
    for which in range(2):
        def drain(d, carry):
            tile_copy(which, lax.rem(line + d, lines)).wait_send()
            return carry

        lax.fori_loop(1, lines, drain, 0)


def deliver(*refs):
    stores = [pltpu.make_async_copy(refs[i], refs[3 + i], refs[6].at[i]) for i in range(3)]
    for store in stores:
        store.start()
    for store in stores:
        store.wait()


def on_device(n, nb, band_block, band_basis, mass_scale, cell_matrices, cell_nodes, cell_count, send_index):
    columns, owned = band_block.shape
    cell_slots, corners = cell_nodes.shape
    width, slots = send_index.shape[1:]
    cols = band_basis.shape[1]
    rows = cols * nb // n
    count = cell_slots * corners
    ghosts = width * slots
    total = owned + ghosts
    group = math.gcd(2, n // nb)
    teams = n // group
    per_seat = n // nb // group
    folds = math.gcd(2, per_seat)
    lines = teams // folds
    per_line = per_seat // folds
    wide = -(-(columns + 3 + width) // 128) * 128
    packed = rows % 128 == 64 and columns % 32 == 0
    folded = ghosts == 64 and columns % 32 == 0
    tile_shape = (columns * rows // 128, 128) if packed else (columns, rows)
    edge_shape = (columns // 2, 128) if folded else (columns, ghosts)
    sent = routes(width // 2, slots)[1]
    anywhere = pl.BlockSpec(memory_space=pl.ANY)
    smem = pl.BlockSpec(memory_space=pltpu.SMEM)
    semaphores = pltpu.SemaphoreType.DMA
    filtered, inter, ham = pl.pallas_call(
        functools.partial(kernel, n, nb, group, packed, folded),
        out_shape=(
            pltpu.VMEM((columns, owned), bf16),
            pltpu.VMEM((columns, rows), f32),
            pltpu.VMEM((columns, rows), f32),
        ),
        in_specs=[anywhere] * 5 + [smem, anywhere],
        out_specs=(pl.BlockSpec(memory_space=pltpu.VMEM),) * 3,
        scratch_shapes=[
            pltpu.VMEM((columns, owned), bf16),
            pltpu.VMEM((owned, cols), bf16),
            pltpu.VMEM((1, owned), f32),
            pltpu.VMEM((cell_slots, corners * corners), bf16),
            pltpu.VMEM((cell_slots, corners), jnp.int32),
            pltpu.VMEM(send_index.shape, jnp.int32),
            pltpu.VMEM((group, nb, per_line, total, folds * rows), bf16),
            pltpu.VMEM((group, per_line, owned, folds * rows), bf16),
            pltpu.VMEM((group, per_line, ghosts, folds * rows), bf16),
            pltpu.VMEM((group, per_line, ghosts, folds * rows), bf16),
            pltpu.VMEM((count, corners), bf16),
            pltpu.VMEM((total, count), bf16),
            pltpu.VMEM((total, count), bf16),
            pltpu.VMEM((total, total), bf16),
            pltpu.VMEM((sent + total, total), bf16),
            pltpu.VMEM((ghosts, wide), bf16),
            pltpu.VMEM((ghosts, wide), bf16),
            pltpu.VMEM((3, sent, columns), bf16),
            pltpu.VMEM((3, sent, columns), bf16),
            pltpu.VMEM((2, group, columns, owned), bf16),
            pltpu.VMEM((2, group) + edge_shape, bf16),
            pltpu.VMEM((2, lines, folds) + tile_shape, f32),
            pltpu.VMEM((2, lines, folds) + tile_shape, bf16),
            pltpu.VMEM((2, lines, folds) + tile_shape, bf16),
            pltpu.VMEM((2, lines) + tile_shape, bf16),
            pltpu.VMEM((2,) + tile_shape, f32),
            pltpu.VMEM((2, lines) + tile_shape, bf16),
            semaphores((6,)),
            semaphores((width,)),
            semaphores((width,)),
            semaphores((3, 2 * width)),
            semaphores((3, 2 * width)),
            semaphores((width,)),
            semaphores((width,)),
            semaphores((2, group, nb, per_line)),
            semaphores((2, group, nb, per_line)),
            semaphores((2, group)),
            semaphores((2, group)),
            semaphores((2, group)),
            semaphores((2, group)),
            semaphores((2, lines, folds)),
            semaphores((2, lines, folds)),
            semaphores((2, lines)),
            semaphores((2, lines)),
        ],
        compiler_params=pltpu.CompilerParams(collective_id=0, has_side_effects=True, vmem_limit_bytes=60 << 20),
    )(
        band_block,
        band_basis,
        mass_scale.reshape(1, owned),
        cell_matrices,
        cell_nodes,
        cell_count,
        send_index,
    )
    results = tuple(pltpu.with_memory_space_constraint(v, pltpu.VMEM) for v in (filtered, inter, ham))
    filtered, inter, ham = pl.pallas_call(
        deliver,
        out_shape=tuple(jax.ShapeDtypeStruct(v.shape, v.dtype) for v in results),
        in_specs=[pl.BlockSpec(memory_space=pltpu.VMEM)] * 3,
        out_specs=(anywhere,) * 3,
        scratch_shapes=[semaphores((3,))],
        compiler_params=pltpu.CompilerParams(vmem_limit_bytes=60 << 20),
    )(*results)
    return filtered, inter.T, ham.T


def solution(mesh):
    placed = (
        P("band", "mesh"),
        P("mesh", "band"),
        P("mesh"),
        P("mesh", None),
        P("mesh", None),
        P("mesh"),
        P("mesh", None, None),
    )
    return jax.shard_map(
        functools.partial(on_device, mesh.shape["mesh"], mesh.shape["band"]),
        mesh=mesh,
        in_specs=placed,
        out_specs=(P("band", "mesh"), P("mesh", "band"), P("mesh", "band")),
        check_vma=False,
    )
```

```python
import functools
import math
import jax
import jax.numpy as jnp
from jax import lax
from jax.experimental import pallas as pl
from jax.experimental.pallas import tpu as pltpu
from jax.sharding import PartitionSpec as P

filter_centre = 1.5
filter_half = 2.5
first_sigma = -0.625
MESH = pl.DeviceIdType.MESH
bf16 = jnp.bfloat16
f32 = jnp.float32


def sigma_values():
    values = [first_sigma]
    for _ in range(2):
        values.append(1.0 / (2.0 / first_sigma - values[-1]))
    return values


def neighbour_offset(neighbour, reach):
    if neighbour < reach:
        return neighbour + 1
    return reach - 1 - neighbour


def dot(a, b):
    return jnp.dot(a, b, preferred_element_type=f32)


def dot_nt(a, b):
    return lax.dot_general(a, b, (((1,), (1,)), ((), ())), preferred_element_type=f32)


def routes(reach, slots):
    width = 2 * reach
    offs = [neighbour_offset(k, reach) for k in range(width)]
    found, row = [], 0
    for d in [sign * distance for distance in range(1, width + 1) for sign in (1, -1)]:
        pieces = []
        for k in range(width):
            if offs[k] == d:
                pieces += [("own", k, 0), ("back", k, 0)]
            pieces += [("third", k, j) for j in range(width) if offs[k] + offs[j] == d]
        found.append((d, row, [(row + slots * i, *piece) for i, piece in enumerate(pieces)]))
        row += slots * len(pieces)
    return found, row, row + slots * len(found)


def kernel(
    n, nb, group, packed, folded, x_hbm, basis_hbm, mass_hbm, mats_hbm, nodes_hbm, count_ref, send_hbm,
    f_ref, inter_ref, ham_ref,
    x_ref, block, mass_ref, mats_ref, nodes_ref, send_ref,
    full, perm, ghost_out, ghost_in, mats, hots, coupled, stiff, stack, intro_out, intro, out, landed,
    held, edge, summed, tile, across, merged, kept, got,
    load_sem, intro_send, intro_recv, halo_send, halo_recv, gb_send, gb_recv, basis_send, basis_recv,
    held_send, held_recv, edge_send, edge_recv,
    cross_send, cross_recv, tile_send, tile_recv,
):
    me = lax.axis_index("mesh")
    mine = lax.axis_index("band")
    seat = lax.rem(me, group)
    team = me // group
    teams = n // group
    folds = math.gcd(2, n // nb // group)
    lines = teams // folds
    line, side = team // folds, lax.rem(team, folds)
    columns, owned = x_ref.shape
    width, slots = send_ref.shape[1:]
    reach = width // 2
    rows = inter_ref.shape[1]
    per_band = n // nb
    per_seat = per_band // group
    per_line = per_seat // folds
    left = rows - rows % 128 if packed else 0
    ghosts = width * slots
    total = owned + ghosts
    cells, corners = nodes_ref.shape
    wide = intro.shape[1]
    plan, sent, packets = routes(reach, slots)
    whole = columns - columns % 128
    rest = columns - whole
    repeats = 128 // rest

    barrier = pltpu.get_barrier_semaphore()

    def greet(d, carry):
        pl.semaphore_signal(
            barrier, inc=1, device_id=(lax.rem(me + d, n), mine), device_id_type=MESH
        )
        return carry

    lax.fori_loop(1, n, greet, 0)
    for d in range(1, nb):
        for e in range(group):
            pl.semaphore_signal(
                barrier,
                inc=1,
                device_id=(team * group + lax.rem(seat + e, group), lax.rem(mine + d, nb)),
                device_id_type=MESH,
            )

    loads = [
        pltpu.make_async_copy(source, target, load_sem.at[i])
        for i, (source, target) in enumerate((
            (send_hbm, send_ref), (mass_hbm, mass_ref), (x_hbm, x_ref), (basis_hbm, block),
            (mats_hbm, mats_ref), (nodes_hbm, nodes_ref),
        ))
    ]
    for load in loads:
        load.start()
    def remote(source, target, send, recv, device):
        return pltpu.make_async_remote_copy(
            src_ref=source, dst_ref=target, send_sem=send, recv_sem=recv,
            device_id=device, device_id_type=MESH,
        )

    def partition(d):
        return (lax.rem(me + d + n, n), mine)

    def beside(e, d):
        return (team * group + lax.rem(seat + e, group), lax.rem(mine + d, nb))

    parts = (pl.ds(0, owned), pl.ds(owned, ghosts))
    ready = (perm, ghost_in)

    def basis_copy(part, e, d, q):
        source = ready[part].at[lax.rem(seat + e, group), q]
        target = full.at[seat, mine, q, parts[part]]
        if e == 0 and d == 0:
            return pltpu.make_async_copy(source, target, basis_recv.at[part, e, d, q])
        return remote(source, target, basis_send.at[part, e, d, q], basis_recv.at[part, e, d, q], beside(e, d))

    def basis_wait(d, q):
        for part in range(2):
            for e in range(group):
                if e == 0 and d == 0:
                    basis_copy(part, e, d, q).wait()
                    continue
                target = full.at[lax.rem(seat + group - e, group), lax.rem(mine + nb - d, nb), q, parts[part]]
                remote(ready[part].at[0, q], target, basis_send.at[part, e, d, q],
                       basis_recv.at[part, e, d, q], beside(e, d)).wait_recv()

    def basis_out(part, bands, q):
        for d in bands:
            for e in range(group):
                if e == 0 and d == 0:
                    basis_copy(part, e, d, q).start()
                else:
                    launch([basis_copy(part, e, d, q)])

    for load in loads[:3]:
        load.wait()
    owned_ids = lax.broadcasted_iota(jnp.int32, (owned, slots), 0)
    hot_parts = [
        jnp.where(owned_ids == send_ref[0, k : k + 1, :], 1.0, 0.0) for k in range(width)
    ]
    send_hot_f = jnp.concatenate(hot_parts, axis=1)
    send_hot_t = send_hot_f.astype(bf16)
    send_hot = send_hot_f.T.astype(bf16)

    mass_row = mass_ref[...]
    high = mass_row.astype(bf16).astype(f32)
    middle = (mass_row - high).astype(bf16).astype(f32)
    low = mass_row - high - middle
    level = lax.broadcasted_iota(jnp.int32, (8, owned), 0)
    extra = jnp.where(level == 0, high, jnp.where(level == 1, middle, jnp.where(level == 2, low, 0.0)))
    raised = jnp.concatenate(
        [x_ref[...].astype(f32), extra, jnp.zeros((wide - columns - 8, owned), f32)], axis=0
    ).T
    raised_f, raised = raised, raised.astype(bf16)
    first_id = columns + 3
    lane = lax.broadcasted_iota(jnp.int32, (ghosts, wide), 1)
    message = dot(send_hot, raised)
    numbers = dot(
        send_hot, (lax.broadcasted_iota(jnp.int32, (owned, wide), 0) + 1).astype(f32).astype(bf16)
    )
    for j in range(width):
        tiled = jnp.concatenate([numbers[j * slots : (j + 1) * slots]] * width, axis=0)
        message = jnp.where(lane == first_id + j, tiled, message)
    intro_out[...] = message.astype(bf16)
    mass_own = jnp.broadcast_to(mass_row, (8, owned)).T[:, :1]

    loads[3].wait()
    for s in range(group):
        for q in range(per_line):
            starts = [(s + group * (q * folds + t)) * rows for t in range(folds)]
            spans = [(a, a + left) for a in starts if left] + [(a + left, a + rows) for a in starts]
            perm[s, q] = jnp.concatenate([block[:, a:b] for a, b in spans], axis=1)
            ghost_out[s, q] = dot(send_hot, perm[s, q]).astype(bf16)

    pl.semaphore_wait(barrier, n - 1 + (nb - 1) * group)

    def halo(source, target, send, recv, cut):
        return [
            remote(cut(source, k), cut(target, (k + reach) % width), send.at[k], recv.at[(k + reach) % width],
                   partition(neighbour_offset(k, reach)))
            for k in range(width)
        ]

    started = []

    def launch(copies):
        for copy in copies:
            copy.start()
        started.extend(copies)

    intros = halo(intro_out, intro, intro_send, intro_recv, lambda ref, k: ref.at[pl.ds(k * slots, slots)])
    launch(intros)
    rims = halo(ghost_out, ghost_in, gb_send, gb_recv, lambda ref, k: ref.at[:, :, pl.ds(k * slots, slots)])
    launch(rims)
    def after_send(index):
        far = range(1, nb)
        if index == 0:
            basis_out(0, far, 0)
            for q in range(per_line):
                basis_out(0, range(1), q)
        if index == 1:
            for copy in rims:
                copy.wait_recv()
            basis_out(1, far, 0)
            for q in range(1, per_line):
                basis_out(0, far, q)
                basis_out(1, far, q)
            for q in range(per_line):
                basis_out(1, range(1), q)

    after_send(0)

    for load in loads[4:]:
        load.wait()
    fold = 128 // corners
    strips = corners // fold
    stacked = jnp.concatenate([mats_ref[:, a * 128 : (a + 1) * 128] for a in range(strips)], axis=0)
    row = lax.broadcasted_iota(jnp.int32, (cells * corners, cells * strips), 0)
    column = lax.broadcasted_iota(jnp.int32, (cells * corners, cells * strips), 1)
    picked = (row % corners) // fold * cells + row // corners == column
    spread = dot(jnp.where(picked, 1.0, 0.0).astype(bf16), stacked)
    turn = lax.broadcasted_iota(jnp.int32, (cells * corners, corners), 0) % fold
    unfolded = spread[:, :corners]
    for a in range(1, fold):
        unfolded = jnp.where(turn == a, spread[:, a * corners : (a + 1) * corners], unfolded)
    mats[...] = unfolded.astype(bf16)

    live = count_ref[0]
    total_ids = lax.broadcasted_iota(jnp.int32, (total, corners), 0)
    for c in range(cells):
        hot = jnp.where(
            jnp.logical_and(total_ids == nodes_ref[c : c + 1, :], c < live), 1.0, 0.0
        ).astype(bf16)
        part = slice(c * corners, (c + 1) * corners)
        hots[:, part] = hot
        coupled[:, part] = dot_nt(hot, mats[part, :]).astype(bf16)
    stiff[...] = dot_nt(hots[...], coupled[...]).astype(bf16)

    own_rows = dot(send_hot, stiff[:owned, :]).astype(bf16)
    for _, _, pieces in plan:
        for row, kind, k, _ in pieces:
            if kind == "own":
                stack[row : row + slots, :] = own_rows[k * slots : (k + 1) * slots]
            if kind == "back":
                stack[row : row + slots, :] = stiff[owned + k * slots : owned + (k + 1) * slots, :]
    stack[sent + ghosts :, :] = stiff[:owned, :]

    for copy in intros:
        copy.wait_recv()
    there = intro[...].astype(f32)
    turned = there.T
    mass_ghost = there[:, columns : columns + 1] + there[:, columns + 1 : columns + 2] + there[:, columns + 2 : columns + 3]
    mass = jnp.concatenate([mass_own, mass_ghost], axis=0)
    slot_lane = lax.broadcasted_iota(jnp.int32, (1, ghosts), 1)
    listed = jnp.zeros((1, ghosts), f32)
    for k in range(width):
        at = first_id + (k + reach) % width
        inside = jnp.logical_and(slot_lane >= k * slots, slot_lane < (k + 1) * slots)
        listed = jnp.where(inside, turned[at : at + 1, :], listed)
    piece_lane = lax.broadcasted_iota(jnp.int32, (slots, ghosts), 1)
    mixers = []
    for k in range(width):
        inside = jnp.logical_and(piece_lane >= k * slots, piece_lane < (k + 1) * slots)
        for j in range(width):
            column = there[k * slots : (k + 1) * slots, first_id + j : first_id + j + 1]
            mixers.append(jnp.where(jnp.logical_and(inside, column == listed), 1.0, 0.0))
    mixed = dot(jnp.concatenate(mixers, axis=0).astype(bf16), stiff[owned:, :]).astype(bf16)

    def mixed_rows(k, j):
        return mixed[(k * width + j) * slots : (k * width + j + 1) * slots]

    for _, _, pieces in plan:
        for row, kind, k, j in pieces:
            if kind == "third":
                stack[row : row + slots, :] = mixed_rows(k, j)
    for k in range(width):
        stack[sent + k * slots : sent + (k + 1) * slots, :] = mixed_rows(k, (k + reach) % width)

    def held_copies(which, e, owner):
        return [
            remote(ref.at[which, owner], ref.at[which, owner], send.at[which, e], recv.at[which, e], beside(e, 0))
            for ref, send, recv in ((held, held_send, held_recv), (edge, edge_send, edge_recv))
        ]

    def share_field(which, inner, outer):
        held[which, seat] = inner.T.astype(bf16)
        outer = outer.T
        if folded:
            outer = jnp.concatenate([outer[: columns // 2], outer[columns // 2 :]], axis=1)
        edge[which, seat] = outer.astype(bf16)
        for e in range(1, group):
            launch(held_copies(which, e, seat))

    def field(which, i):
        outer = edge[which, i]
        if folded:
            outer = jnp.concatenate([outer[:, :ghosts], outer[:, ghosts:]], axis=0)
        return jnp.concatenate([held[which, i], outer], axis=1)

    def pack(value, t):
        at = folds * left + t * (rows - left)
        ends = value[:, at : at + rows - left]
        if not packed:
            return ends
        half = columns // 2
        parts = [value[:, t * left + a : t * left + a + 128] for a in range(0, left, 128)]
        return jnp.concatenate(parts + [jnp.concatenate([ends[:half], ends[half:]], axis=1)], axis=0)

    def unpack(value):
        if not packed:
            return value
        full_parts = rows // 128
        parts = [value[a * columns : (a + 1) * columns] for a in range(full_parts)]
        rest = value[full_parts * columns :]
        parts.append(jnp.concatenate([rest[:, :64], rest[:, 64:]], axis=0))
        return jnp.concatenate(parts, axis=1)

    chunks = [(d, q) for q in range(per_line) for d in range(nb)]
    chunks.sort(key=lambda chunk: chunk[0] > 0)
    late = [chunk for chunk in chunks if chunk[0] > 0 and chunk[1] == per_line - 1]
    early = [chunk for chunk in chunks if chunk not in late]

    def target_line(d, q):
        return lax.rem(mine + nb - d, nb) * per_line + q

    def cross_copy(which, d, q, f):
        to = target_line(d, q)
        there = lax.rem(side + f, folds)
        return remote(tile.at[which, to, there], across.at[which, to, f], cross_send.at[which, to, f],
                      cross_recv.at[which, to, f], ((line * folds + there) * group + seat, mine))

    def tile_copy(which, to):
        return remote(merged.at[which, to], got.at[which, line], tile_send.at[which, to],
                      tile_recv.at[which, line], ((to * folds + side) * group + seat, mine))

    def fields_in(which):
        for e in range(1, group):
            for copy in held_copies(which, e, lax.rem(seat + group - e, group)):
                copy.wait_recv()

    def begin(which, some):
        own = field(which, seat)
        return {(d, q): dot(own, full[seat, lax.rem(mine + nb - d, nb), q]) for d, q in some}

    def multiply(which, some, begun=None):
        begun = begun or begin(which, some)
        others = [lax.rem(seat + e, group) for e in range(1, group)]
        fields = [field(which, i) for i in others]
        for d, q in some:
            band, to = lax.rem(mine + nb - d, nb), target_line(d, q)
            value = begun[d, q]
            for i, other in zip(others, fields):
                value = value + dot(other, full[i, band, q])
            for t in range(folds):
                part = pack(value, t)
                summed[which, to, t] = part
                tile[which, to, t] = part.astype(bf16)
            launch([cross_copy(which, d, q, f) for f in range(1, folds)])

    def tiles_on(which, some):
        for d, q in some:
            to = target_line(d, q)
            acc = summed[which, to, side]
            for f in range(1, folds):
                cross_copy(which, d, q, f).wait_recv()
                acc = acc + across[which, to, f].astype(f32)
            merged[which, to] = acc.astype(bf16)

            @pl.when(to != line)
            def _():
                tile_copy(which, to).start()

            @pl.when(to == line)
            def _():
                kept[which] = acc

    def tiles_in(which):
        def collect(d, acc):
            source = lax.rem(line + d, lines)
            remote(merged.at[which, source], got.at[which, source], tile_send.at[which, source],
                   tile_recv.at[which, source], ((source * folds + side) * group + seat, mine)).wait_recv()
            return acc + got[which, source].astype(f32)

        return unpack(lax.fori_loop(1, lines, collect, kept[which], unroll=lines <= 4))

    sigmas = sigma_values()
    start = jnp.concatenate([raised_f, there], axis=0)
    previous = current = jnp.concatenate(
        [start[:, :whole]] + [start[:, whole:columns]] * repeats, axis=1
    ).astype(bf16)
    strip = lax.broadcasted_iota(jnp.int32, (slots, 128), 1) // rest

    def repeat(value):
        shift = rest
        while shift < 128:
            value = value + pltpu.roll(value, shift, 1)
            shift *= 2
        return value

    for step in range(3):
        scaled = (mass * current.astype(f32)).astype(bf16)
        leaving = dot(stack[:sent, :], scaled)
        copies = []
        base_row = 0
        for index, (d, row, pieces) in enumerate(plan):
            size = slots * len(pieces)
            out[step, base_row : base_row + size] = leaving[row : row + size, :whole].astype(bf16)
            ends = leaving[row : row + slots, whole:]
            for i in range(1, len(pieces)):
                ends = jnp.where(strip == i, leaving[row + i * slots : row + (i + 1) * slots, whole:], ends)
            out[step, base_row + size : base_row + size + slots, :128] = ends.astype(bf16)
            span = pl.ds(base_row, size + slots)
            copies.append(
                remote(out.at[step, span], landed.at[step, span], halo_send.at[step, index],
                       halo_recv.at[step, index], partition(d))
            )
            launch(copies[-1:])
            base_row += size + slots
        local = dot(stack[sent:, :], scaled)
        if step == 0:
            scale_now, mixing = sigmas[0] / filter_half, 0.0
        else:
            scale_now, mixing = 2.0 * sigmas[step] / filter_half, sigmas[step - 1] * sigmas[step]
        after_send(step + 1)
        base = -(filter_centre * scale_now) * current.astype(f32)
        if step > 0:
            base = base - mixing * previous.astype(f32)
        if step == 2:
            ends = {}
            for _, _, pieces in plan:
                for row, kind, k, _ in pieces:
                    if kind == "back":
                        ends[k] = leaving[row : row + slots]
            outer = jnp.concatenate([ends[k] for k in range(width)], axis=0)
            share_field(
                0,
                (scale_now * mass_own * local[ghosts:] + base[:owned])[:, :columns],
                (scale_now * mass_ghost * outer)[:, :columns],
            )
            for chunk in early:
                basis_wait(*chunk)
            begun = begin(0, early)
            fields_in(0)
            for chunk in early:
                multiply(0, [chunk], begun)
        for copy in copies:
            copy.wait_recv()
        arrived = landed[step].astype(f32)
        ghost_sums = [local[k * slots : (k + 1) * slots, :whole] for k in range(width)]
        ghost_ends = [jnp.zeros((slots, 128), f32)] * width
        backs, back_ends = [None] * width, [None] * width
        base_row = 0
        for _, _, pieces in plan:
            edge_row = base_row + slots * len(pieces)
            ends = arrived[edge_row : edge_row + slots, :128]
            for i, (_, kind, k, j) in enumerate(pieces):
                at = base_row + i * slots
                end = jnp.where(strip == i, ends, 0.0)
                if kind == "back":
                    backs[(k + reach) % width] = landed[step, at : at + slots]
                    back_ends[(k + reach) % width] = end
                    continue
                block_k = ((k if kind == "own" else j) + reach) % width
                ghost_sums[block_k] += arrived[at : at + slots]
                ghost_ends[block_k] += end
            base_row = edge_row + slots
        returned = jnp.concatenate(
            [jnp.concatenate(backs, axis=0), repeat(jnp.concatenate(back_ends, axis=0)).astype(bf16)], axis=1
        )
        inner = local[ghosts:] + dot(send_hot_t, returned)
        ghost_sums = [
            jnp.concatenate(
                [ghost_sums[k], local[k * slots : (k + 1) * slots, whole:] + repeat(ghost_ends[k])], axis=1
            )
            for k in range(width)
        ]
        sums = jnp.concatenate([inner] + ghost_sums, axis=0)
        previous, current = current, (scale_now * (mass * sums) + base).astype(bf16)

    scaled = (mass * current.astype(f32)).astype(bf16)
    image = mass * dot(stiff[...], scaled)
    share_field(1, image[:owned, :columns], image[owned:, :columns])
    f_ref[...] = current[:owned, :columns].astype(f32).T.astype(bf16)
    begun = begin(1, early)
    fields_in(1)
    multiply(1, early[:1], begun)
    tiles_on(0, early[:1])
    multiply(1, early[1:2], begun)
    tiles_on(0, early[1:2])
    multiply(1, early[2:], begun)
    tiles_on(0, early[2:])
    for chunk in late:
        basis_wait(*chunk)
    multiply(1, late)
    multiply(0, late)
    tiles_on(1, early)
    tiles_on(1, late)
    tiles_on(0, late)
    inter_ref[...] = tiles_in(0)
    ham_ref[...] = tiles_in(1)

    for copy in started:
        copy.wait_send()
    for which in range(2):
        def drain(d, carry):
            tile_copy(which, lax.rem(line + d, lines)).wait_send()
            return carry

        lax.fori_loop(1, lines, drain, 0)


def deliver(*refs):
    stores = [pltpu.make_async_copy(refs[i], refs[3 + i], refs[6].at[i]) for i in range(3)]
    for store in stores:
        store.start()
    for store in stores:
        store.wait()


def on_device(n, nb, band_block, band_basis, mass_scale, cell_matrices, cell_nodes, cell_count, send_index):
    columns, owned = band_block.shape
    cell_slots, corners = cell_nodes.shape
    width, slots = send_index.shape[1:]
    cols = band_basis.shape[1]
    rows = cols * nb // n
    count = cell_slots * corners
    ghosts = width * slots
    total = owned + ghosts
    group = math.gcd(2, n // nb)
    teams = n // group
    per_seat = n // nb // group
    folds = math.gcd(2, per_seat)
    lines = teams // folds
    per_line = per_seat // folds
    wide = -(-(columns + 3 + width) // 128) * 128
    packed = rows % 128 == 64 and columns % 32 == 0
    folded = ghosts == 64 and columns % 32 == 0
    tile_shape = (columns * rows // 128, 128) if packed else (columns, rows)
    edge_shape = (columns // 2, 128) if folded else (columns, ghosts)
    _, sent, packets = routes(width // 2, slots)
    anywhere = pl.BlockSpec(memory_space=pl.ANY)
    smem = pl.BlockSpec(memory_space=pltpu.SMEM)
    semaphores = pltpu.SemaphoreType.DMA
    filtered, inter, ham = pl.pallas_call(
        functools.partial(kernel, n, nb, group, packed, folded),
        out_shape=(
            pltpu.VMEM((columns, owned), bf16),
            pltpu.VMEM((columns, rows), f32),
            pltpu.VMEM((columns, rows), f32),
        ),
        in_specs=[anywhere] * 5 + [smem, anywhere],
        out_specs=(pl.BlockSpec(memory_space=pltpu.VMEM),) * 3,
        scratch_shapes=[
            pltpu.VMEM((columns, owned), bf16),
            pltpu.VMEM((owned, cols), bf16),
            pltpu.VMEM((1, owned), f32),
            pltpu.VMEM((cell_slots, corners * corners), bf16),
            pltpu.VMEM((cell_slots, corners), jnp.int32),
            pltpu.VMEM(send_index.shape, jnp.int32),
            pltpu.VMEM((group, nb, per_line, total, folds * rows), bf16),
            pltpu.VMEM((group, per_line, owned, folds * rows), bf16),
            pltpu.VMEM((group, per_line, ghosts, folds * rows), bf16),
            pltpu.VMEM((group, per_line, ghosts, folds * rows), bf16),
            pltpu.VMEM((count, corners), bf16),
            pltpu.VMEM((total, count), bf16),
            pltpu.VMEM((total, count), bf16),
            pltpu.VMEM((total, total), bf16),
            pltpu.VMEM((sent + total, total), bf16),
            pltpu.VMEM((ghosts, wide), bf16),
            pltpu.VMEM((ghosts, wide), bf16),
            pltpu.VMEM((3, packets, columns - columns % 128), bf16),
            pltpu.VMEM((3, packets, columns - columns % 128), bf16),
            pltpu.VMEM((2, group, columns, owned), bf16),
            pltpu.VMEM((2, group) + edge_shape, bf16),
            pltpu.VMEM((2, lines, folds) + tile_shape, f32),
            pltpu.VMEM((2, lines, folds) + tile_shape, bf16),
            pltpu.VMEM((2, lines, folds) + tile_shape, bf16),
            pltpu.VMEM((2, lines) + tile_shape, bf16),
            pltpu.VMEM((2,) + tile_shape, f32),
            pltpu.VMEM((2, lines) + tile_shape, bf16),
            semaphores((6,)),
            semaphores((width,)),
            semaphores((width,)),
            semaphores((3, 2 * width)),
            semaphores((3, 2 * width)),
            semaphores((width,)),
            semaphores((width,)),
            semaphores((2, group, nb, per_line)),
            semaphores((2, group, nb, per_line)),
            semaphores((2, group)),
            semaphores((2, group)),
            semaphores((2, group)),
            semaphores((2, group)),
            semaphores((2, lines, folds)),
            semaphores((2, lines, folds)),
            semaphores((2, lines)),
            semaphores((2, lines)),
        ],
        compiler_params=pltpu.CompilerParams(collective_id=0, has_side_effects=True, vmem_limit_bytes=60 << 20),
    )(
        band_block,
        band_basis,
        mass_scale.reshape(1, owned),
        cell_matrices,
        cell_nodes,
        cell_count,
        send_index,
    )
    results = tuple(pltpu.with_memory_space_constraint(v, pltpu.VMEM) for v in (filtered, inter, ham))
    filtered, inter, ham = pl.pallas_call(
        deliver,
        out_shape=tuple(jax.ShapeDtypeStruct(v.shape, v.dtype) for v in results),
        in_specs=[pl.BlockSpec(memory_space=pltpu.VMEM)] * 3,
        out_specs=(anywhere,) * 3,
        scratch_shapes=[semaphores((3,))],
        compiler_params=pltpu.CompilerParams(vmem_limit_bytes=60 << 20),
    )(*results)
    return filtered, inter.T, ham.T


def solution(mesh):
    placed = (
        P("band", "mesh"),
        P("mesh", "band"),
        P("mesh"),
        P("mesh", None),
        P("mesh", None),
        P("mesh"),
        P("mesh", None, None),
    )
    return jax.shard_map(
        functools.partial(on_device, mesh.shape["mesh"], mesh.shape["band"]),
        mesh=mesh,
        in_specs=placed,
        out_specs=(P("band", "mesh"), P("mesh", "band"), P("mesh", "band")),
        check_vma=False,
    )
```

```python
import functools
import math
import jax
import jax.numpy as jnp
from jax import lax
from jax.experimental import pallas as pl
from jax.experimental.pallas import tpu as pltpu
from jax.sharding import PartitionSpec as P

filter_centre = 1.5
filter_half = 2.5
first_sigma = -0.625
MESH = pl.DeviceIdType.MESH
bf16 = jnp.bfloat16
f32 = jnp.float32


def sigma_values():
    values = [first_sigma]
    for _ in range(2):
        values.append(1.0 / (2.0 / first_sigma - values[-1]))
    return values


def neighbour_offset(neighbour, reach):
    if neighbour < reach:
        return neighbour + 1
    return reach - 1 - neighbour


def dot(a, b):
    return jnp.dot(a, b, preferred_element_type=f32)


def dot_nt(a, b):
    return lax.dot_general(a, b, (((1,), (1,)), ((), ())), preferred_element_type=f32)


def routes(reach, slots):
    width = 2 * reach
    offs = [neighbour_offset(k, reach) for k in range(width)]
    found, row = [], 0
    for d in [sign * distance for distance in range(1, width + 1) for sign in (1, -1)]:
        pieces = []
        for k in range(width):
            if offs[k] == d:
                pieces += [("own", k, 0), ("back", k, 0)]
            pieces += [("third", k, j) for j in range(width) if offs[k] + offs[j] == d]
        found.append((d, row, [(row + slots * i, *piece) for i, piece in enumerate(pieces)]))
        row += slots * len(pieces)
    return found, row, row + slots * len(found)


def kernel(
    n, nb, group, packed, folded, x_hbm, basis_hbm, mass_hbm, mats_hbm, nodes_hbm, count_ref, send_hbm,
    f_ref, inter_ref, ham_ref,
    x_ref, block, mass_ref, mats_ref, nodes_ref, send_ref,
    full, perm, ghost_out, ghost_in, mats, hots, coupled, stiff, stack, intro_out, intro, out, landed,
    held, edge, summed, tile, across, merged, kept, got,
    load_sem, intro_send, intro_recv, halo_send, halo_recv, gb_send, gb_recv, basis_send, basis_recv,
    held_send, held_recv, edge_send, edge_recv,
    cross_send, cross_recv, tile_send, tile_recv,
):
    me = lax.axis_index("mesh")
    mine = lax.axis_index("band")
    seat = lax.rem(me, group)
    team = me // group
    teams = n // group
    folds = math.gcd(2, n // nb // group)
    lines = teams // folds
    line, side = team // folds, lax.rem(team, folds)
    columns, owned = x_ref.shape
    width, slots = send_ref.shape[1:]
    reach = width // 2
    rows = inter_ref.shape[1]
    per_band = n // nb
    per_seat = per_band // group
    per_line = per_seat // folds
    left = rows - rows % 128 if packed else 0
    ghosts = width * slots
    total = owned + ghosts
    cells, corners = nodes_ref.shape
    wide = intro.shape[1]
    plan, sent, packets = routes(reach, slots)
    whole = columns - columns % 128
    rest = columns - whole
    repeats = 128 // rest

    barrier = pltpu.get_barrier_semaphore()

    met = [d % n for v in range(1, width + 1) for d in (v, -v)]
    met += [d for d in range(group * folds, n, group * folds)]
    met += [d % n for v in range(1, group * folds) for d in (v, -v)]
    met = list(dict.fromkeys(met))
    for d in met:
        pl.semaphore_signal(
            barrier, inc=1, device_id=(lax.rem(me + d, n), mine), device_id_type=MESH
        )
    for d in range(1, nb):
        for e in range(group):
            pl.semaphore_signal(
                barrier,
                inc=1,
                device_id=(team * group + lax.rem(seat + e, group), lax.rem(mine + d, nb)),
                device_id_type=MESH,
            )

    loads = [
        pltpu.make_async_copy(source, target, load_sem.at[i])
        for i, (source, target) in enumerate((
            (send_hbm, send_ref), (mass_hbm, mass_ref), (x_hbm, x_ref), (basis_hbm, block),
            (mats_hbm, mats_ref), (nodes_hbm, nodes_ref),
        ))
    ]
    for load in loads:
        load.start()
    def remote(source, target, send, recv, device):
        return pltpu.make_async_remote_copy(
            src_ref=source, dst_ref=target, send_sem=send, recv_sem=recv,
            device_id=device, device_id_type=MESH,
        )

    def partition(d):
        return (lax.rem(me + d + n, n), mine)

    def beside(e, d):
        return (team * group + lax.rem(seat + e, group), lax.rem(mine + d, nb))

    parts = (pl.ds(0, owned), pl.ds(owned, ghosts))
    ready = (perm, ghost_in)

    def basis_copy(part, e, d, q):
        source = ready[part].at[lax.rem(seat + e, group), q]
        target = full.at[seat, mine, q, parts[part]]
        if e == 0 and d == 0:
            return pltpu.make_async_copy(source, target, basis_recv.at[part, e, d, q])
        return remote(source, target, basis_send.at[part, e, d, q], basis_recv.at[part, e, d, q], beside(e, d))

    def basis_wait(d, q):
        for part in range(2):
            for e in range(group):
                if e == 0 and d == 0:
                    basis_copy(part, e, d, q).wait()
                    continue
                target = full.at[lax.rem(seat + group - e, group), lax.rem(mine + nb - d, nb), q, parts[part]]
                remote(ready[part].at[0, q], target, basis_send.at[part, e, d, q],
                       basis_recv.at[part, e, d, q], beside(e, d)).wait_recv()

    def basis_out(part, bands, q):
        for d in bands:
            for e in range(group):
                if e == 0 and d == 0:
                    basis_copy(part, e, d, q).start()
                else:
                    launch([basis_copy(part, e, d, q)])

    for load in loads[:3]:
        load.wait()
    owned_ids = lax.broadcasted_iota(jnp.int32, (owned, slots), 0)
    hot_parts = [
        jnp.where(owned_ids == send_ref[0, k : k + 1, :], 1.0, 0.0) for k in range(width)
    ]
    send_hot_f = jnp.concatenate(hot_parts, axis=1)
    send_hot_t = send_hot_f.astype(bf16)
    send_hot = send_hot_f.T.astype(bf16)

    mass_row = mass_ref[...]
    high = mass_row.astype(bf16).astype(f32)
    middle = (mass_row - high).astype(bf16).astype(f32)
    low = mass_row - high - middle
    level = lax.broadcasted_iota(jnp.int32, (8, owned), 0)
    extra = jnp.where(level == 0, high, jnp.where(level == 1, middle, jnp.where(level == 2, low, 0.0)))
    raised = jnp.concatenate(
        [x_ref[...].astype(f32), extra, jnp.zeros((wide - columns - 8, owned), f32)], axis=0
    ).T
    raised_f, raised = raised, raised.astype(bf16)
    first_id = columns + 3
    lane = lax.broadcasted_iota(jnp.int32, (ghosts, wide), 1)
    message = dot(send_hot, raised)
    numbers = dot(
        send_hot, (lax.broadcasted_iota(jnp.int32, (owned, wide), 0) + 1).astype(f32).astype(bf16)
    )
    for j in range(width):
        tiled = jnp.concatenate([numbers[j * slots : (j + 1) * slots]] * width, axis=0)
        message = jnp.where(lane == first_id + j, tiled, message)
    intro_out[...] = message.astype(bf16)
    mass_own = jnp.broadcast_to(mass_row, (8, owned)).T[:, :1]

    loads[3].wait()
    for s in range(group):
        for q in range(per_line):
            starts = [(s + group * (q * folds + t)) * rows for t in range(folds)]
            spans = [(a, a + left) for a in starts if left] + [(a + left, a + rows) for a in starts]
            perm[s, q] = jnp.concatenate([block[:, a:b] for a, b in spans], axis=1)
            ghost_out[s, q] = dot(send_hot, perm[s, q]).astype(bf16)

    pl.semaphore_wait(barrier, len(met) + (nb - 1) * group)

    def halo(source, target, send, recv, cut):
        return [
            remote(cut(source, k), cut(target, (k + reach) % width), send.at[k], recv.at[(k + reach) % width],
                   partition(neighbour_offset(k, reach)))
            for k in range(width)
        ]

    started = []

    def launch(copies):
        for copy in copies:
            copy.start()
        started.extend(copies)

    intros = halo(intro_out, intro, intro_send, intro_recv, lambda ref, k: ref.at[pl.ds(k * slots, slots)])
    launch(intros)
    rims = halo(ghost_out, ghost_in, gb_send, gb_recv, lambda ref, k: ref.at[:, :, pl.ds(k * slots, slots)])
    order = [lax.rem(line + 1 + i, per_line) for i in range(per_line)]
    def after_send(index):
        far = range(1, nb)
        if index == 0:
            basis_out(0, far, order[0])
            launch(rims)
            for q in order:
                basis_out(0, range(1), q)
        if index == 1:
            for copy in rims:
                copy.wait_recv()
            basis_out(1, far, order[0])
            for q in order[1:]:
                basis_out(0, far, q)
                basis_out(1, far, q)
            for q in order:
                basis_out(1, range(1), q)

    after_send(0)

    for load in loads[4:]:
        load.wait()
    fold = 128 // corners
    strips = corners // fold
    stacked = jnp.concatenate([mats_ref[:, a * 128 : (a + 1) * 128] for a in range(strips)], axis=0)
    row = lax.broadcasted_iota(jnp.int32, (cells * corners, cells * strips), 0)
    column = lax.broadcasted_iota(jnp.int32, (cells * corners, cells * strips), 1)
    picked = (row % corners) // fold * cells + row // corners == column
    spread = dot(jnp.where(picked, 1.0, 0.0).astype(bf16), stacked)
    turn = lax.broadcasted_iota(jnp.int32, (cells * corners, corners), 0) % fold
    unfolded = spread[:, :corners]
    for a in range(1, fold):
        unfolded = jnp.where(turn == a, spread[:, a * corners : (a + 1) * corners], unfolded)
    mats[...] = unfolded.astype(bf16)

    live = count_ref[0]
    total_ids = lax.broadcasted_iota(jnp.int32, (total, corners), 0)
    for c in range(cells):
        hot = jnp.where(
            jnp.logical_and(total_ids == nodes_ref[c : c + 1, :], c < live), 1.0, 0.0
        ).astype(bf16)
        part = slice(c * corners, (c + 1) * corners)
        hots[:, part] = hot
        coupled[:, part] = dot_nt(hot, mats[part, :]).astype(bf16)
    stiff[...] = dot_nt(hots[...], coupled[...]).astype(bf16)

    own_rows = dot(send_hot, stiff[:owned, :]).astype(bf16)
    for _, _, pieces in plan:
        for row, kind, k, _ in pieces:
            if kind == "own":
                stack[row : row + slots, :] = own_rows[k * slots : (k + 1) * slots]
            if kind == "back":
                stack[row : row + slots, :] = stiff[owned + k * slots : owned + (k + 1) * slots, :]
    stack[sent + ghosts :, :] = stiff[:owned, :]

    for copy in intros:
        copy.wait_recv()
    there = intro[...].astype(f32)
    turned = there.T
    mass_ghost = there[:, columns : columns + 1] + there[:, columns + 1 : columns + 2] + there[:, columns + 2 : columns + 3]
    mass = jnp.concatenate([mass_own, mass_ghost], axis=0)
    slot_lane = lax.broadcasted_iota(jnp.int32, (1, ghosts), 1)
    listed = jnp.zeros((1, ghosts), f32)
    for k in range(width):
        at = first_id + (k + reach) % width
        inside = jnp.logical_and(slot_lane >= k * slots, slot_lane < (k + 1) * slots)
        listed = jnp.where(inside, turned[at : at + 1, :], listed)
    piece_lane = lax.broadcasted_iota(jnp.int32, (slots, ghosts), 1)
    mixers = []
    for k in range(width):
        inside = jnp.logical_and(piece_lane >= k * slots, piece_lane < (k + 1) * slots)
        for j in range(width):
            column = there[k * slots : (k + 1) * slots, first_id + j : first_id + j + 1]
            mixers.append(jnp.where(jnp.logical_and(inside, column == listed), 1.0, 0.0))
    mixed = dot(jnp.concatenate(mixers, axis=0).astype(bf16), stiff[owned:, :]).astype(bf16)

    def mixed_rows(k, j):
        return mixed[(k * width + j) * slots : (k * width + j + 1) * slots]

    for _, _, pieces in plan:
        for row, kind, k, j in pieces:
            if kind == "third":
                stack[row : row + slots, :] = mixed_rows(k, j)
    for k in range(width):
        stack[sent + k * slots : sent + (k + 1) * slots, :] = mixed_rows(k, (k + reach) % width)

    def held_copies(which, e, owner):
        return [
            remote(ref.at[which, owner], ref.at[which, owner], send.at[which, e], recv.at[which, e], beside(e, 0))
            for ref, send, recv in ((held, held_send, held_recv), (edge, edge_send, edge_recv))
        ]

    def share_field(which, inner, outer):
        held[which, seat] = inner.T.astype(bf16)
        outer = outer.T
        if folded:
            outer = jnp.concatenate([outer[: columns // 2], outer[columns // 2 :]], axis=1)
        edge[which, seat] = outer.astype(bf16)
        for e in range(1, group):
            launch(held_copies(which, e, seat))

    def field(which, i):
        outer = edge[which, i]
        if folded:
            outer = jnp.concatenate([outer[:, :ghosts], outer[:, ghosts:]], axis=0)
        return jnp.concatenate([held[which, i], outer], axis=1)

    def pack(value, t):
        at = folds * left + t * (rows - left)
        ends = value[:, at : at + rows - left]
        if not packed:
            return ends
        half = columns // 2
        parts = [value[:, t * left + a : t * left + a + 128] for a in range(0, left, 128)]
        return jnp.concatenate(parts + [jnp.concatenate([ends[:half], ends[half:]], axis=1)], axis=0)

    def unpack(value):
        if not packed:
            return value
        full_parts = rows // 128
        parts = [value[a * columns : (a + 1) * columns] for a in range(full_parts)]
        rest = value[full_parts * columns :]
        parts.append(jnp.concatenate([rest[:, :64], rest[:, 64:]], axis=0))
        return jnp.concatenate(parts, axis=1)

    early = [(d, q) for q in order[:-1] for d in range(nb)] + [(0, order[-1])]
    late = [(d, order[-1]) for d in range(1, nb)]
    own_band = lax.rem(mine + nb - line // per_line, nb)
    sooner = early[:-1]
    later = [(lax.rem(own_band + 1 + i, nb), order[-1]) for i in range(nb)]

    def target_line(d, q):
        return lax.rem(mine + nb - d, nb) * per_line + q

    def cross_copy(which, d, q, f):
        to = target_line(d, q)
        there = lax.rem(side + f, folds)
        return remote(tile.at[which, to, there], across.at[which, to, f], cross_send.at[which, to, f],
                      cross_recv.at[which, to, f], ((line * folds + there) * group + seat, mine))

    def tile_copy(which, to):
        return remote(merged.at[which, to], got.at[which, line], tile_send.at[which, to],
                      tile_recv.at[which, line], ((to * folds + side) * group + seat, mine))

    def fields_in(which):
        for e in range(1, group):
            for copy in held_copies(which, e, lax.rem(seat + group - e, group)):
                copy.wait_recv()

    def begin(which, some):
        own = field(which, seat)
        return [dot(own, full[seat, lax.rem(mine + nb - d, nb), q]) for d, q in some]

    def multiply(which, some, begun=None):
        begun = begun or begin(which, some)
        others = [lax.rem(seat + e, group) for e in range(1, group)]
        fields = [field(which, i) for i in others]
        for (d, q), value in zip(some, begun):
            band, to = lax.rem(mine + nb - d, nb), target_line(d, q)
            for i, other in zip(others, fields):
                value = value + dot(other, full[i, band, q])
            for t in range(folds):
                part = pack(value, t)
                summed[which, to, t] = part
                tile[which, to, t] = part.astype(bf16)
            launch([cross_copy(which, d, q, f) for f in range(1, folds)])

    def tiles_on(which, some):
        for d, q in some:
            to = target_line(d, q)
            acc = summed[which, to, side]
            for f in range(1, folds):
                cross_copy(which, d, q, f).wait_recv()
                acc = acc + across[which, to, f].astype(f32)
            merged[which, to] = acc.astype(bf16)

            @pl.when(to != line)
            def _():
                tile_copy(which, to).start()

            @pl.when(to == line)
            def _():
                kept[which] = acc

    def tiles_in(which):
        def collect(d, acc):
            source = lax.rem(line + d, lines)
            remote(merged.at[which, source], got.at[which, source], tile_send.at[which, source],
                   tile_recv.at[which, source], ((source * folds + side) * group + seat, mine)).wait_recv()
            return acc + got[which, source].astype(f32)

        return unpack(lax.fori_loop(1, lines, collect, kept[which], unroll=lines <= 4))

    sigmas = sigma_values()
    start = jnp.concatenate([raised_f, there], axis=0)
    previous = current = jnp.concatenate(
        [start[:, :whole]] + [start[:, whole:columns]] * repeats, axis=1
    ).astype(bf16)
    strip = lax.broadcasted_iota(jnp.int32, (slots, 128), 1) // rest

    def repeat(value):
        shift = rest
        while shift < 128:
            value = value + pltpu.roll(value, shift, 1)
            shift *= 2
        return value

    for step in range(3):
        scaled = (mass * current.astype(f32)).astype(bf16)
        leaving = dot(stack[:sent, :], scaled)
        copies = []
        base_row = 0
        for index, (d, row, pieces) in enumerate(plan):
            size = slots * len(pieces)
            out[step, base_row : base_row + size] = leaving[row : row + size, :whole].astype(bf16)
            ends = leaving[row : row + slots, whole:]
            for i in range(1, len(pieces)):
                ends = jnp.where(strip == i, leaving[row + i * slots : row + (i + 1) * slots, whole:], ends)
            out[step, base_row + size : base_row + size + slots, :128] = ends.astype(bf16)
            span = pl.ds(base_row, size + slots)
            copies.append(
                remote(out.at[step, span], landed.at[step, span], halo_send.at[step, index],
                       halo_recv.at[step, index], partition(d))
            )
            launch(copies[-1:])
            base_row += size + slots
        local = dot(stack[sent:, :], scaled)
        if step == 0:
            scale_now, mixing = sigmas[0] / filter_half, 0.0
        else:
            scale_now, mixing = 2.0 * sigmas[step] / filter_half, sigmas[step - 1] * sigmas[step]
        after_send(step + 1)
        base = -(filter_centre * scale_now) * current.astype(f32)
        if step > 0:
            base = base - mixing * previous.astype(f32)
        if step == 2:
            ends = {}
            for _, _, pieces in plan:
                for row, kind, k, _ in pieces:
                    if kind == "back":
                        ends[k] = leaving[row : row + slots]
            outer = jnp.concatenate([ends[k] for k in range(width)], axis=0)
            share_field(
                0,
                (scale_now * mass_own * local[ghosts:] + base[:owned])[:, :columns],
                (scale_now * mass_ghost * outer)[:, :columns],
            )
            for chunk in early:
                basis_wait(*chunk)
            begun = begin(0, early)
            fields_in(0)
            multiply(0, early, begun)
        for copy in copies:
            copy.wait_recv()
        arrived = landed[step].astype(f32)
        ghost_sums = [local[k * slots : (k + 1) * slots, :whole] for k in range(width)]
        ghost_ends = [jnp.zeros((slots, 128), f32)] * width
        backs, back_ends = [None] * width, [None] * width
        base_row = 0
        for _, _, pieces in plan:
            edge_row = base_row + slots * len(pieces)
            ends = arrived[edge_row : edge_row + slots, :128]
            for i, (_, kind, k, j) in enumerate(pieces):
                at = base_row + i * slots
                end = jnp.where(strip == i, ends, 0.0)
                if kind == "back":
                    backs[(k + reach) % width] = landed[step, at : at + slots]
                    back_ends[(k + reach) % width] = end
                    continue
                block_k = ((k if kind == "own" else j) + reach) % width
                ghost_sums[block_k] += arrived[at : at + slots]
                ghost_ends[block_k] += end
            base_row = edge_row + slots
        returned = jnp.concatenate(
            [jnp.concatenate(backs, axis=0), repeat(jnp.concatenate(back_ends, axis=0)).astype(bf16)], axis=1
        )
        inner = local[ghosts:] + dot(send_hot_t, returned)
        ghost_sums = [
            jnp.concatenate(
                [ghost_sums[k], local[k * slots : (k + 1) * slots, whole:] + repeat(ghost_ends[k])], axis=1
            )
            for k in range(width)
        ]
        sums = jnp.concatenate([inner] + ghost_sums, axis=0)
        previous, current = current, (scale_now * (mass * sums) + base).astype(bf16)

    scaled = (mass * current.astype(f32)).astype(bf16)
    image = mass * dot(stiff[...], scaled)
    share_field(1, image[:owned, :columns], image[owned:, :columns])
    f_ref[...] = current[:owned, :columns].astype(f32).T.astype(bf16)
    begun = begin(1, sooner)
    fields_in(1)
    multiply(1, sooner[:1], begun[:1])
    tiles_on(0, early[:1])
    multiply(1, sooner[1:], begun[1:])
    tiles_on(0, early[1:])
    for chunk in late:
        basis_wait(*chunk)
    multiply(1, later)
    multiply(0, late)
    tiles_on(1, sooner)
    tiles_on(1, later)
    tiles_on(0, late)
    inter_ref[...] = tiles_in(0)
    ham_ref[...] = tiles_in(1)

    for copy in started:
        copy.wait_send()
    for which in range(2):
        def drain(d, carry):
            tile_copy(which, lax.rem(line + d, lines)).wait_send()
            return carry

        lax.fori_loop(1, lines, drain, 0)


def deliver(*refs):
    stores = [pltpu.make_async_copy(refs[i], refs[3 + i], refs[6].at[i]) for i in range(3)]
    for store in stores:
        store.start()
    for store in stores:
        store.wait()


def on_device(n, nb, band_block, band_basis, mass_scale, cell_matrices, cell_nodes, cell_count, send_index):
    columns, owned = band_block.shape
    cell_slots, corners = cell_nodes.shape
    width, slots = send_index.shape[1:]
    cols = band_basis.shape[1]
    rows = cols * nb // n
    count = cell_slots * corners
    ghosts = width * slots
    total = owned + ghosts
    group = math.gcd(2, n // nb)
    teams = n // group
    per_seat = n // nb // group
    folds = math.gcd(2, per_seat)
    lines = teams // folds
    per_line = per_seat // folds
    wide = -(-(columns + 3 + width) // 128) * 128
    packed = rows % 128 == 64 and columns % 32 == 0
    folded = ghosts == 64 and columns % 32 == 0
    tile_shape = (columns * rows // 128, 128) if packed else (columns, rows)
    edge_shape = (columns // 2, 128) if folded else (columns, ghosts)
    _, sent, packets = routes(width // 2, slots)
    anywhere = pl.BlockSpec(memory_space=pl.ANY)
    smem = pl.BlockSpec(memory_space=pltpu.SMEM)
    semaphores = pltpu.SemaphoreType.DMA
    filtered, inter, ham = pl.pallas_call(
        functools.partial(kernel, n, nb, group, packed, folded),
        out_shape=(
            pltpu.VMEM((columns, owned), bf16),
            pltpu.VMEM((columns, rows), f32),
            pltpu.VMEM((columns, rows), f32),
        ),
        in_specs=[anywhere] * 5 + [smem, anywhere],
        out_specs=(pl.BlockSpec(memory_space=pltpu.VMEM),) * 3,
        scratch_shapes=[
            pltpu.VMEM((columns, owned), bf16),
            pltpu.VMEM((owned, cols), bf16),
            pltpu.VMEM((1, owned), f32),
            pltpu.VMEM((cell_slots, corners * corners), bf16),
            pltpu.VMEM((cell_slots, corners), jnp.int32),
            pltpu.VMEM(send_index.shape, jnp.int32),
            pltpu.VMEM((group, nb, per_line, total, folds * rows), bf16),
            pltpu.VMEM((group, per_line, owned, folds * rows), bf16),
            pltpu.VMEM((group, per_line, ghosts, folds * rows), bf16),
            pltpu.VMEM((group, per_line, ghosts, folds * rows), bf16),
            pltpu.VMEM((count, corners), bf16),
            pltpu.VMEM((total, count), bf16),
            pltpu.VMEM((total, count), bf16),
            pltpu.VMEM((total, total), bf16),
            pltpu.VMEM((sent + total, total), bf16),
            pltpu.VMEM((ghosts, wide), bf16),
            pltpu.VMEM((ghosts, wide), bf16),
            pltpu.VMEM((3, packets, columns - columns % 128), bf16),
            pltpu.VMEM((3, packets, columns - columns % 128), bf16),
            pltpu.VMEM((2, group, columns, owned), bf16),
            pltpu.VMEM((2, group) + edge_shape, bf16),
            pltpu.VMEM((2, lines, folds) + tile_shape, f32),
            pltpu.VMEM((2, lines, folds) + tile_shape, bf16),
            pltpu.VMEM((2, lines, folds) + tile_shape, bf16),
            pltpu.VMEM((2, lines) + tile_shape, bf16),
            pltpu.VMEM((2,) + tile_shape, f32),
            pltpu.VMEM((2, lines) + tile_shape, bf16),
            semaphores((6,)),
            semaphores((width,)),
            semaphores((width,)),
            semaphores((3, 2 * width)),
            semaphores((3, 2 * width)),
            semaphores((width,)),
            semaphores((width,)),
            semaphores((2, group, nb, per_line)),
            semaphores((2, group, nb, per_line)),
            semaphores((2, group)),
            semaphores((2, group)),
            semaphores((2, group)),
            semaphores((2, group)),
            semaphores((2, lines, folds)),
            semaphores((2, lines, folds)),
            semaphores((2, lines)),
            semaphores((2, lines)),
        ],
        compiler_params=pltpu.CompilerParams(collective_id=0, has_side_effects=True, vmem_limit_bytes=60 << 20),
    )(
        band_block,
        band_basis,
        mass_scale.reshape(1, owned),
        cell_matrices,
        cell_nodes,
        cell_count,
        send_index,
    )
    results = tuple(pltpu.with_memory_space_constraint(v, pltpu.VMEM) for v in (filtered, inter, ham))
    filtered, inter, ham = pl.pallas_call(
        deliver,
        out_shape=tuple(jax.ShapeDtypeStruct(v.shape, v.dtype) for v in results),
        in_specs=[pl.BlockSpec(memory_space=pltpu.VMEM)] * 3,
        out_specs=(anywhere,) * 3,
        scratch_shapes=[semaphores((3,))],
        compiler_params=pltpu.CompilerParams(vmem_limit_bytes=60 << 20),
    )(*results)
    return filtered, inter.T, ham.T


def solution(mesh):
    placed = (
        P("band", "mesh"),
        P("mesh", "band"),
        P("mesh"),
        P("mesh", None),
        P("mesh", None),
        P("mesh"),
        P("mesh", None, None),
    )
    return jax.shard_map(
        functools.partial(on_device, mesh.shape["mesh"], mesh.shape["band"]),
        mesh=mesh,
        in_specs=placed,
        out_specs=(P("band", "mesh"), P("mesh", "band"), P("mesh", "band")),
        check_vma=False,
    )
```

```python
import functools
import math
import jax
import jax.numpy as jnp
from jax import lax
from jax.experimental import pallas as pl
from jax.experimental.pallas import tpu as pltpu
from jax.sharding import PartitionSpec as P

filter_centre = 1.5
filter_half = 2.5
first_sigma = -0.625
MESH = pl.DeviceIdType.MESH
bf16 = jnp.bfloat16
f32 = jnp.float32


def sigma_values():
    values = [first_sigma]
    for _ in range(2):
        values.append(1.0 / (2.0 / first_sigma - values[-1]))
    return values


def neighbour_offset(neighbour, reach):
    if neighbour < reach:
        return neighbour + 1
    return reach - 1 - neighbour


def dot(a, b):
    return jnp.dot(a, b, preferred_element_type=f32)


def dot_nt(a, b):
    return lax.dot_general(a, b, (((1,), (1,)), ((), ())), preferred_element_type=f32)


def routes(reach, slots):
    width = 2 * reach
    offs = [neighbour_offset(k, reach) for k in range(width)]
    found, row = [], 0
    for d in [sign * distance for distance in range(1, width + 1) for sign in (1, -1)]:
        pieces = []
        for k in range(width):
            if offs[k] == d:
                pieces += [("own", k, 0), ("back", k, 0)]
            pieces += [("third", k, j) for j in range(width) if offs[k] + offs[j] == d]
        found.append((d, row, [(row + slots * i, *piece) for i, piece in enumerate(pieces)]))
        row += slots * len(pieces)
    return found, row, row + slots * len(found)


def kernel(
    n, nb, group, packed, folded, x_hbm, basis_hbm, mass_hbm, mats_hbm, nodes_hbm, count_ref, send_hbm,
    f_ref, inter_ref, ham_ref,
    x_ref, block, mass_ref, mats_ref, nodes_ref, send_ref,
    full, perm, ghost_out, ghost_in, mats, hots, coupled, stiff, stack, intro_out, intro, out, landed,
    held, edge, summed, tile, across, merged, kept, got,
    load_sem, intro_send, intro_recv, halo_send, halo_recv, gb_send, gb_recv, basis_send, basis_recv,
    held_send, held_recv, edge_send, edge_recv,
    cross_send, cross_recv, tile_send, tile_recv,
):
    me = lax.axis_index("mesh")
    mine = lax.axis_index("band")
    seat = lax.rem(me, group)
    team = me // group
    teams = n // group
    folds = math.gcd(2, n // nb // group)
    lines = teams // folds
    line, side = team // folds, lax.rem(team, folds)
    columns, owned = x_ref.shape
    width, slots = send_ref.shape[1:]
    reach = width // 2
    rows = inter_ref.shape[1]
    per_band = n // nb
    per_seat = per_band // group
    per_line = per_seat // folds
    left = rows - rows % 128 if packed else 0
    ghosts = width * slots
    total = owned + ghosts
    cells, corners = nodes_ref.shape
    wide = intro.shape[1]
    plan, sent, packets = routes(reach, slots)
    whole = columns - columns % 128
    rest = columns - whole
    repeats = 128 // rest

    barrier = pltpu.get_barrier_semaphore()

    met = [d % n for v in range(1, width + 1) for d in (v, -v)]
    met += [d for d in range(group * folds, n, group * folds)]
    met += [d % n for v in range(1, group * folds) for d in (v, -v)]
    met = list(dict.fromkeys(met))
    for d in met:
        pl.semaphore_signal(
            barrier, inc=1, device_id=(lax.rem(me + d, n), mine), device_id_type=MESH
        )
    for d in range(1, nb):
        for e in range(group):
            pl.semaphore_signal(
                barrier,
                inc=1,
                device_id=(team * group + lax.rem(seat + e, group), lax.rem(mine + d, nb)),
                device_id_type=MESH,
            )

    loads = [
        pltpu.make_async_copy(source, target, load_sem.at[i])
        for i, (source, target) in enumerate((
            (send_hbm, send_ref), (mass_hbm, mass_ref), (x_hbm, x_ref), (basis_hbm, block),
            (mats_hbm, mats_ref), (nodes_hbm, nodes_ref),
        ))
    ]
    for load in loads:
        load.start()
    def remote(source, target, send, recv, device):
        return pltpu.make_async_remote_copy(
            src_ref=source, dst_ref=target, send_sem=send, recv_sem=recv,
            device_id=device, device_id_type=MESH,
        )

    def partition(d):
        return (lax.rem(me + d + n, n), mine)

    def beside(e, d):
        return (team * group + lax.rem(seat + e, group), lax.rem(mine + d, nb))

    parts = (pl.ds(0, owned), pl.ds(owned, ghosts))
    ready = (perm, ghost_in)

    def basis_copy(part, e, d, q):
        source = ready[part].at[lax.rem(seat + e, group), q]
        target = full.at[seat, mine, q, parts[part]]
        if e == 0 and d == 0:
            return pltpu.make_async_copy(source, target, basis_recv.at[part, e, d, q])
        return remote(source, target, basis_send.at[part, e, d, q], basis_recv.at[part, e, d, q], beside(e, d))

    def basis_wait(d, q):
        for part in range(2):
            for e in range(group):
                if e == 0 and d == 0:
                    basis_copy(part, e, d, q).wait()
                    continue
                target = full.at[lax.rem(seat + group - e, group), lax.rem(mine + nb - d, nb), q, parts[part]]
                remote(ready[part].at[0, q], target, basis_send.at[part, e, d, q],
                       basis_recv.at[part, e, d, q], beside(e, d)).wait_recv()

    def basis_out(part, bands, q):
        for d in bands:
            for e in range(group):
                if e == 0 and d == 0:
                    basis_copy(part, e, d, q).start()
                else:
                    launch([basis_copy(part, e, d, q)])

    for load in loads[:3]:
        load.wait()
    owned_ids = lax.broadcasted_iota(jnp.int32, (owned, slots), 0)
    hot_parts = [
        jnp.where(owned_ids == send_ref[0, k : k + 1, :], 1.0, 0.0) for k in range(width)
    ]
    send_hot_f = jnp.concatenate(hot_parts, axis=1)
    send_hot_t = send_hot_f.astype(bf16)
    send_hot = send_hot_f.T.astype(bf16)

    mass_row = mass_ref[...]
    high = mass_row.astype(bf16).astype(f32)
    middle = (mass_row - high).astype(bf16).astype(f32)
    low = mass_row - high - middle
    level = lax.broadcasted_iota(jnp.int32, (8, owned), 0)
    extra = jnp.where(level == 0, high, jnp.where(level == 1, middle, jnp.where(level == 2, low, 0.0)))
    raised = jnp.concatenate(
        [x_ref[...].astype(f32), extra, jnp.zeros((wide - columns - 8, owned), f32)], axis=0
    ).T
    raised_f, raised = raised, raised.astype(bf16)
    first_id = columns + 3
    lane = lax.broadcasted_iota(jnp.int32, (ghosts, wide), 1)
    message = dot(send_hot, raised)
    numbers = dot(
        send_hot, (lax.broadcasted_iota(jnp.int32, (owned, wide), 0) + 1).astype(f32).astype(bf16)
    )
    for j in range(width):
        tiled = jnp.concatenate([numbers[j * slots : (j + 1) * slots]] * width, axis=0)
        message = jnp.where(lane == first_id + j, tiled, message)
    intro_out[...] = message.astype(bf16)
    mass_own = jnp.broadcast_to(mass_row, (8, owned)).T[:, :1]

    pl.semaphore_wait(barrier, len(met) + (nb - 1) * group)

    def halo(source, target, send, recv, cut):
        return [
            remote(cut(source, k), cut(target, (k + reach) % width), send.at[k], recv.at[(k + reach) % width],
                   partition(neighbour_offset(k, reach)))
            for k in range(width)
        ]

    started = []

    def launch(copies):
        for copy in copies:
            copy.start()
        started.extend(copies)

    intros = halo(intro_out, intro, intro_send, intro_recv, lambda ref, k: ref.at[pl.ds(k * slots, slots)])
    launch(intros)
    loads[3].wait()
    for s in range(group):
        for q in range(per_line):
            starts = [(s + group * (q * folds + t)) * rows for t in range(folds)]
            spans = [(a, a + left) for a in starts if left] + [(a + left, a + rows) for a in starts]
            perm[s, q] = jnp.concatenate([block[:, a:b] for a, b in spans], axis=1)
            ghost_out[s, q] = dot(send_hot, perm[s, q]).astype(bf16)
    rims = halo(ghost_out, ghost_in, gb_send, gb_recv, lambda ref, k: ref.at[:, :, pl.ds(k * slots, slots)])
    order = [lax.rem(line + 1 + i, per_line) for i in range(per_line)]
    def after_send(index):
        far = range(1, nb)
        if index == 0:
            basis_out(0, far, order[0])
            launch(rims)
            for q in order:
                basis_out(0, range(1), q)
        if index == 1:
            for copy in rims:
                copy.wait_recv()
            basis_out(1, far, order[0])
            for q in order[1:]:
                basis_out(0, far, q)
                basis_out(1, far, q)
            for q in order:
                basis_out(1, range(1), q)

    after_send(0)

    for load in loads[4:]:
        load.wait()
    fold = 128 // corners
    strips = corners // fold
    stacked = jnp.concatenate([mats_ref[:, a * 128 : (a + 1) * 128] for a in range(strips)], axis=0)
    row = lax.broadcasted_iota(jnp.int32, (cells * corners, cells * strips), 0)
    column = lax.broadcasted_iota(jnp.int32, (cells * corners, cells * strips), 1)
    picked = (row % corners) // fold * cells + row // corners == column
    spread = dot(jnp.where(picked, 1.0, 0.0).astype(bf16), stacked)
    turn = lax.broadcasted_iota(jnp.int32, (cells * corners, corners), 0) % fold
    unfolded = spread[:, :corners]
    for a in range(1, fold):
        unfolded = jnp.where(turn == a, spread[:, a * corners : (a + 1) * corners], unfolded)
    mats[...] = unfolded.astype(bf16)

    live = count_ref[0]
    total_ids = lax.broadcasted_iota(jnp.int32, (total, corners), 0)
    for c in range(cells):
        hot = jnp.where(
            jnp.logical_and(total_ids == nodes_ref[c : c + 1, :], c < live), 1.0, 0.0
        ).astype(bf16)
        part = slice(c * corners, (c + 1) * corners)
        hots[:, part] = hot
        coupled[:, part] = dot_nt(hot, mats[part, :]).astype(bf16)
    stiff[...] = dot_nt(hots[...], coupled[...]).astype(bf16)

    own_rows = dot(send_hot, stiff[:owned, :]).astype(bf16)
    for _, _, pieces in plan:
        for row, kind, k, _ in pieces:
            if kind == "own":
                stack[row : row + slots, :] = own_rows[k * slots : (k + 1) * slots]
            if kind == "back":
                stack[row : row + slots, :] = stiff[owned + k * slots : owned + (k + 1) * slots, :]
    stack[sent + ghosts :, :] = stiff[:owned, :]

    for copy in intros:
        copy.wait_recv()
    there = intro[...].astype(f32)
    turned = there.T
    mass_ghost = there[:, columns : columns + 1] + there[:, columns + 1 : columns + 2] + there[:, columns + 2 : columns + 3]
    mass = jnp.concatenate([mass_own, mass_ghost], axis=0)
    slot_lane = lax.broadcasted_iota(jnp.int32, (1, ghosts), 1)
    listed = jnp.zeros((1, ghosts), f32)
    for k in range(width):
        at = first_id + (k + reach) % width
        inside = jnp.logical_and(slot_lane >= k * slots, slot_lane < (k + 1) * slots)
        listed = jnp.where(inside, turned[at : at + 1, :], listed)
    piece_lane = lax.broadcasted_iota(jnp.int32, (slots, ghosts), 1)
    mixers = []
    for k in range(width):
        inside = jnp.logical_and(piece_lane >= k * slots, piece_lane < (k + 1) * slots)
        for j in range(width):
            column = there[k * slots : (k + 1) * slots, first_id + j : first_id + j + 1]
            mixers.append(jnp.where(jnp.logical_and(inside, column == listed), 1.0, 0.0))
    mixed = dot(jnp.concatenate(mixers, axis=0).astype(bf16), stiff[owned:, :]).astype(bf16)

    def mixed_rows(k, j):
        return mixed[(k * width + j) * slots : (k * width + j + 1) * slots]

    for _, _, pieces in plan:
        for row, kind, k, j in pieces:
            if kind == "third":
                stack[row : row + slots, :] = mixed_rows(k, j)
    for k in range(width):
        stack[sent + k * slots : sent + (k + 1) * slots, :] = mixed_rows(k, (k + reach) % width)

    def held_copies(which, e, owner):
        return [
            remote(ref.at[which, owner], ref.at[which, owner], send.at[which, e], recv.at[which, e], beside(e, 0))
            for ref, send, recv in ((held, held_send, held_recv), (edge, edge_send, edge_recv))
        ]

    def share_field(which, inner, outer):
        held[which, seat] = inner.T.astype(bf16)
        outer = outer.T
        if folded:
            outer = jnp.concatenate([outer[: columns // 2], outer[columns // 2 :]], axis=1)
        edge[which, seat] = outer.astype(bf16)
        for e in range(1, group):
            launch(held_copies(which, e, seat))

    def field(which, i):
        outer = edge[which, i]
        if folded:
            outer = jnp.concatenate([outer[:, :ghosts], outer[:, ghosts:]], axis=0)
        return jnp.concatenate([held[which, i], outer], axis=1)

    def pack(value, t):
        at = folds * left + t * (rows - left)
        ends = value[:, at : at + rows - left]
        if not packed:
            return ends
        half = columns // 2
        parts = [value[:, t * left + a : t * left + a + 128] for a in range(0, left, 128)]
        return jnp.concatenate(parts + [jnp.concatenate([ends[:half], ends[half:]], axis=1)], axis=0)

    def unpack(value):
        if not packed:
            return value
        full_parts = rows // 128
        parts = [value[a * columns : (a + 1) * columns] for a in range(full_parts)]
        rest = value[full_parts * columns :]
        parts.append(jnp.concatenate([rest[:, :64], rest[:, 64:]], axis=0))
        return jnp.concatenate(parts, axis=1)

    early = [(d, q) for q in order[:-1] for d in range(nb)] + [(0, order[-1])]
    late = [(d, order[-1]) for d in range(1, nb)]
    own_band = lax.rem(mine + nb - line // per_line, nb)
    sooner = early[:-1]
    later = [(lax.rem(own_band + 1 + i, nb), order[-1]) for i in range(nb)]

    def target_line(d, q):
        return lax.rem(mine + nb - d, nb) * per_line + q

    def cross_copy(which, d, q, f):
        to = target_line(d, q)
        there = lax.rem(side + f, folds)
        return remote(tile.at[which, to, there], across.at[which, to, f], cross_send.at[which, to, f],
                      cross_recv.at[which, to, f], ((line * folds + there) * group + seat, mine))

    def tile_copy(which, to):
        return remote(merged.at[which, to], got.at[which, line], tile_send.at[which, to],
                      tile_recv.at[which, line], ((to * folds + side) * group + seat, mine))

    def fields_in(which):
        for e in range(1, group):
            for copy in held_copies(which, e, lax.rem(seat + group - e, group)):
                copy.wait_recv()

    def begin(which, some):
        own = field(which, seat)
        return [dot(own, full[seat, lax.rem(mine + nb - d, nb), q]) for d, q in some]

    def multiply(which, some, begun=None):
        begun = begun or begin(which, some)
        others = [lax.rem(seat + e, group) for e in range(1, group)]
        fields = [field(which, i) for i in others]
        for (d, q), value in zip(some, begun):
            band, to = lax.rem(mine + nb - d, nb), target_line(d, q)
            for i, other in zip(others, fields):
                value = value + dot(other, full[i, band, q])
            for t in range(folds):
                part = pack(value, t)
                summed[which, to, t] = part
                tile[which, to, t] = part.astype(bf16)
            launch([cross_copy(which, d, q, f) for f in range(1, folds)])

    def tiles_on(which, some):
        for d, q in some:
            to = target_line(d, q)
            acc = summed[which, to, side]
            for f in range(1, folds):
                cross_copy(which, d, q, f).wait_recv()
                acc = acc + across[which, to, f].astype(f32)
            merged[which, to] = acc.astype(bf16)

            @pl.when(to != line)
            def _():
                tile_copy(which, to).start()

            @pl.when(to == line)
            def _():
                kept[which] = acc

    def tiles_in(which):
        def collect(d, acc):
            source = lax.rem(line + d, lines)
            remote(merged.at[which, source], got.at[which, source], tile_send.at[which, source],
                   tile_recv.at[which, source], ((source * folds + side) * group + seat, mine)).wait_recv()
            return acc + got[which, source].astype(f32)

        return unpack(lax.fori_loop(1, lines, collect, kept[which], unroll=lines <= 4))

    sigmas = sigma_values()
    start = jnp.concatenate([raised_f, there], axis=0)
    previous = current = jnp.concatenate(
        [start[:, :whole]] + [start[:, whole:columns]] * repeats, axis=1
    ).astype(bf16)
    strip = lax.broadcasted_iota(jnp.int32, (slots, 128), 1) // rest

    def repeat(value):
        shift = rest
        while shift < 128:
            value = value + pltpu.roll(value, shift, 1)
            shift *= 2
        return value

    for step in range(3):
        scaled = (mass * current.astype(f32)).astype(bf16)
        near_rows = plan[width][1]
        leaving = near = dot(stack[:near_rows, :], scaled)
        shift = 0
        copies = []
        base_row = 0
        for index, (d, row, pieces) in enumerate(plan):
            size = slots * len(pieces)
            if row == near_rows:
                leaving, shift = dot(stack[near_rows:sent, :], scaled), near_rows
            row -= shift
            out[step, base_row : base_row + size] = leaving[row : row + size, :whole].astype(bf16)
            ends = leaving[row : row + slots, whole:]
            for i in range(1, len(pieces)):
                ends = jnp.where(strip == i, leaving[row + i * slots : row + (i + 1) * slots, whole:], ends)
            out[step, base_row + size : base_row + size + slots, :128] = ends.astype(bf16)
            span = pl.ds(base_row, size + slots)
            copies.append(
                remote(out.at[step, span], landed.at[step, span], halo_send.at[step, index],
                       halo_recv.at[step, index], partition(d))
            )
            launch(copies[-1:])
            base_row += size + slots
        local = dot(stack[sent:, :], scaled)
        if step == 0:
            scale_now, mixing = sigmas[0] / filter_half, 0.0
        else:
            scale_now, mixing = 2.0 * sigmas[step] / filter_half, sigmas[step - 1] * sigmas[step]
        after_send(step + 1)
        base = -(filter_centre * scale_now) * current.astype(f32)
        if step > 0:
            base = base - mixing * previous.astype(f32)
        if step == 2:
            ends = {}
            for _, _, pieces in plan:
                for row, kind, k, _ in pieces:
                    if kind == "back":
                        ends[k] = near[row : row + slots]
            outer = jnp.concatenate([ends[k] for k in range(width)], axis=0)
            share_field(
                0,
                (scale_now * mass_own * local[ghosts:] + base[:owned])[:, :columns],
                (scale_now * mass_ghost * outer)[:, :columns],
            )
            for chunk in early:
                basis_wait(*chunk)
            begun = begin(0, early)
            fields_in(0)
            multiply(0, early, begun)
        for copy in copies:
            copy.wait_recv()
        arrived = landed[step].astype(f32)
        ghost_sums = [local[k * slots : (k + 1) * slots, :whole] for k in range(width)]
        ghost_ends = [jnp.zeros((slots, 128), f32)] * width
        backs, back_ends = [None] * width, [None] * width
        base_row = 0
        for _, _, pieces in plan:
            edge_row = base_row + slots * len(pieces)
            ends = arrived[edge_row : edge_row + slots, :128]
            for i, (_, kind, k, j) in enumerate(pieces):
                at = base_row + i * slots
                end = jnp.where(strip == i, ends, 0.0)
                if kind == "back":
                    backs[(k + reach) % width] = landed[step, at : at + slots]
                    back_ends[(k + reach) % width] = end
                    continue
                block_k = ((k if kind == "own" else j) + reach) % width
                ghost_sums[block_k] += arrived[at : at + slots]
                ghost_ends[block_k] += end
            base_row = edge_row + slots
        returned = jnp.concatenate(
            [jnp.concatenate(backs, axis=0), repeat(jnp.concatenate(back_ends, axis=0)).astype(bf16)], axis=1
        )
        inner = local[ghosts:] + dot(send_hot_t, returned)
        ghost_sums = [
            jnp.concatenate(
                [ghost_sums[k], local[k * slots : (k + 1) * slots, whole:] + repeat(ghost_ends[k])], axis=1
            )
            for k in range(width)
        ]
        sums = jnp.concatenate([inner] + ghost_sums, axis=0)
        previous, current = current, (scale_now * (mass * sums) + base).astype(bf16)

    scaled = (mass * current.astype(f32)).astype(bf16)
    image = mass * dot(stiff[...], scaled)
    share_field(1, image[:owned, :columns], image[owned:, :columns])
    f_ref[...] = current[:owned, :columns].astype(f32).T.astype(bf16)
    begun = begin(1, sooner)
    fields_in(1)
    multiply(1, sooner[:1], begun[:1])
    tiles_on(0, early[:1])
    multiply(1, sooner[1:], begun[1:])
    tiles_on(0, early[1:])
    for chunk in late:
        basis_wait(*chunk)
    multiply(1, later)
    multiply(0, late)
    tiles_on(1, sooner)
    tiles_on(1, later)
    tiles_on(0, late)
    inter_ref[...] = tiles_in(0)
    ham_ref[...] = tiles_in(1)

    for copy in started:
        copy.wait_send()
    for which in range(2):
        def drain(d, carry):
            tile_copy(which, lax.rem(line + d, lines)).wait_send()
            return carry

        lax.fori_loop(1, lines, drain, 0)


def deliver(*refs):
    stores = [pltpu.make_async_copy(refs[i], refs[3 + i], refs[6].at[i]) for i in range(3)]
    for store in stores:
        store.start()
    for store in stores:
        store.wait()


def on_device(n, nb, band_block, band_basis, mass_scale, cell_matrices, cell_nodes, cell_count, send_index):
    columns, owned = band_block.shape
    cell_slots, corners = cell_nodes.shape
    width, slots = send_index.shape[1:]
    cols = band_basis.shape[1]
    rows = cols * nb // n
    count = cell_slots * corners
    ghosts = width * slots
    total = owned + ghosts
    group = math.gcd(2, n // nb)
    teams = n // group
    per_seat = n // nb // group
    folds = math.gcd(2, per_seat)
    lines = teams // folds
    per_line = per_seat // folds
    wide = -(-(columns + 3 + width) // 128) * 128
    packed = rows % 128 == 64 and columns % 32 == 0
    folded = ghosts == 64 and columns % 32 == 0
    tile_shape = (columns * rows // 128, 128) if packed else (columns, rows)
    edge_shape = (columns // 2, 128) if folded else (columns, ghosts)
    _, sent, packets = routes(width // 2, slots)
    anywhere = pl.BlockSpec(memory_space=pl.ANY)
    smem = pl.BlockSpec(memory_space=pltpu.SMEM)
    semaphores = pltpu.SemaphoreType.DMA
    filtered, inter, ham = pl.pallas_call(
        functools.partial(kernel, n, nb, group, packed, folded),
        out_shape=(
            pltpu.VMEM((columns, owned), bf16),
            pltpu.VMEM((columns, rows), f32),
            pltpu.VMEM((columns, rows), f32),
        ),
        in_specs=[anywhere] * 5 + [smem, anywhere],
        out_specs=(pl.BlockSpec(memory_space=pltpu.VMEM),) * 3,
        scratch_shapes=[
            pltpu.VMEM((columns, owned), bf16),
            pltpu.VMEM((owned, cols), bf16),
            pltpu.VMEM((1, owned), f32),
            pltpu.VMEM((cell_slots, corners * corners), bf16),
            pltpu.VMEM((cell_slots, corners), jnp.int32),
            pltpu.VMEM(send_index.shape, jnp.int32),
            pltpu.VMEM((group, nb, per_line, total, folds * rows), bf16),
            pltpu.VMEM((group, per_line, owned, folds * rows), bf16),
            pltpu.VMEM((group, per_line, ghosts, folds * rows), bf16),
            pltpu.VMEM((group, per_line, ghosts, folds * rows), bf16),
            pltpu.VMEM((count, corners), bf16),
            pltpu.VMEM((total, count), bf16),
            pltpu.VMEM((total, count), bf16),
            pltpu.VMEM((total, total), bf16),
            pltpu.VMEM((sent + total, total), bf16),
            pltpu.VMEM((ghosts, wide), bf16),
            pltpu.VMEM((ghosts, wide), bf16),
            pltpu.VMEM((3, packets, columns - columns % 128), bf16),
            pltpu.VMEM((3, packets, columns - columns % 128), bf16),
            pltpu.VMEM((2, group, columns, owned), bf16),
            pltpu.VMEM((2, group) + edge_shape, bf16),
            pltpu.VMEM((2, lines, folds) + tile_shape, f32),
            pltpu.VMEM((2, lines, folds) + tile_shape, bf16),
            pltpu.VMEM((2, lines, folds) + tile_shape, bf16),
            pltpu.VMEM((2, lines) + tile_shape, bf16),
            pltpu.VMEM((2,) + tile_shape, f32),
            pltpu.VMEM((2, lines) + tile_shape, bf16),
            semaphores((6,)),
            semaphores((width,)),
            semaphores((width,)),
            semaphores((3, 2 * width)),
            semaphores((3, 2 * width)),
            semaphores((width,)),
            semaphores((width,)),
            semaphores((2, group, nb, per_line)),
            semaphores((2, group, nb, per_line)),
            semaphores((2, group)),
            semaphores((2, group)),
            semaphores((2, group)),
            semaphores((2, group)),
            semaphores((2, lines, folds)),
            semaphores((2, lines, folds)),
            semaphores((2, lines)),
            semaphores((2, lines)),
        ],
        compiler_params=pltpu.CompilerParams(collective_id=0, has_side_effects=True, vmem_limit_bytes=60 << 20),
    )(
        band_block,
        band_basis,
        mass_scale.reshape(1, owned),
        cell_matrices,
        cell_nodes,
        cell_count,
        send_index,
    )
    results = tuple(pltpu.with_memory_space_constraint(v, pltpu.VMEM) for v in (filtered, inter, ham))
    filtered, inter, ham = pl.pallas_call(
        deliver,
        out_shape=tuple(jax.ShapeDtypeStruct(v.shape, v.dtype) for v in results),
        in_specs=[pl.BlockSpec(memory_space=pltpu.VMEM)] * 3,
        out_specs=(anywhere,) * 3,
        scratch_shapes=[semaphores((3,))],
        compiler_params=pltpu.CompilerParams(vmem_limit_bytes=60 << 20),
    )(*results)
    return filtered, inter.T, ham.T


def solution(mesh):
    placed = (
        P("band", "mesh"),
        P("mesh", "band"),
        P("mesh"),
        P("mesh", None),
        P("mesh", None),
        P("mesh"),
        P("mesh", None, None),
    )
    return jax.shard_map(
        functools.partial(on_device, mesh.shape["mesh"], mesh.shape["band"]),
        mesh=mesh,
        in_specs=placed,
        out_specs=(P("band", "mesh"), P("mesh", "band"), P("mesh", "band")),
        check_vma=False,
    )
```

```python
import functools
import math
import jax
import jax.numpy as jnp
from jax import lax
from jax.experimental import pallas as pl
from jax.experimental.pallas import tpu as pltpu
from jax.sharding import PartitionSpec as P

filter_centre = 1.5
filter_half = 2.5
first_sigma = -0.625
MESH = pl.DeviceIdType.MESH
bf16 = jnp.bfloat16
f32 = jnp.float32


def sigma_values():
    values = [first_sigma]
    for _ in range(2):
        values.append(1.0 / (2.0 / first_sigma - values[-1]))
    return values


def neighbour_offset(neighbour, reach):
    if neighbour < reach:
        return neighbour + 1
    return reach - 1 - neighbour


def dot(a, b):
    return jnp.dot(a, b, preferred_element_type=f32)


def dot_nt(a, b):
    return lax.dot_general(a, b, (((1,), (1,)), ((), ())), preferred_element_type=f32)


def routes(reach, slots):
    width = 2 * reach
    offs = [neighbour_offset(k, reach) for k in range(width)]
    found, row = [], 0
    for d in [sign * distance for distance in range(1, width + 1) for sign in (1, -1)]:
        pieces = []
        for k in range(width):
            if offs[k] == d:
                pieces += [("own", k, 0), ("back", k, 0)]
            pieces += [("third", k, j) for j in range(width) if offs[k] + offs[j] == d]
        found.append((d, row, [(row + slots * i, *piece) for i, piece in enumerate(pieces)]))
        row += slots * len(pieces)
    return found, row, row + slots * len(found)


def kernel(
    n, nb, group, packed, folded, x_hbm, basis_hbm, mass_hbm, mats_hbm, nodes_hbm, count_ref, send_hbm,
    f_ref, inter_ref, ham_ref,
    x_ref, block, mass_ref, mats_ref, nodes_ref, send_ref,
    full, perm, ghost_out, ghost_in, mats, hots, coupled, stiff, stack, intro_out, intro, out, landed,
    held, edge, summed, tile, across, merged, kept, got,
    load_sem, intro_send, intro_recv, halo_send, halo_recv, gb_send, gb_recv, basis_send, basis_recv,
    held_send, held_recv, edge_send, edge_recv,
    cross_send, cross_recv, tile_send, tile_recv,
):
    me = lax.axis_index("mesh")
    mine = lax.axis_index("band")
    seat = lax.rem(me, group)
    team = me // group
    teams = n // group
    folds = math.gcd(2, n // nb // group)
    lines = teams // folds
    line, side = team // folds, lax.rem(team, folds)
    columns, owned = x_ref.shape
    width, slots = send_ref.shape[1:]
    reach = width // 2
    rows = inter_ref.shape[1]
    per_band = n // nb
    per_seat = per_band // group
    per_line = per_seat // folds
    left = rows - rows % 128 if packed else 0
    ghosts = width * slots
    total = owned + ghosts
    cells, corners = nodes_ref.shape
    wide = intro.shape[1]
    plan, sent, packets = routes(reach, slots)
    whole = columns - columns % 128
    rest = columns - whole
    repeats = 128 // rest

    barrier = pltpu.get_barrier_semaphore()

    met = [d % n for v in range(1, width + 1) for d in (v, -v)]
    met += [d for d in range(group * folds, n, group * folds)]
    met += [d % n for v in range(1, group * folds) for d in (v, -v)]
    met = list(dict.fromkeys(met))
    for d in met:
        pl.semaphore_signal(
            barrier, inc=1, device_id=(lax.rem(me + d, n), mine), device_id_type=MESH
        )
    for d in range(1, nb):
        for e in range(group):
            pl.semaphore_signal(
                barrier,
                inc=1,
                device_id=(team * group + lax.rem(seat + e, group), lax.rem(mine + d, nb)),
                device_id_type=MESH,
            )

    loads = [
        pltpu.make_async_copy(source, target, load_sem.at[i])
        for i, (source, target) in enumerate((
            (send_hbm, send_ref), (mass_hbm, mass_ref), (x_hbm, x_ref), (basis_hbm, block),
            (mats_hbm, mats_ref), (nodes_hbm, nodes_ref),
        ))
    ]
    for load in loads:
        load.start()
    def remote(source, target, send, recv, device):
        return pltpu.make_async_remote_copy(
            src_ref=source, dst_ref=target, send_sem=send, recv_sem=recv,
            device_id=device, device_id_type=MESH,
        )

    def partition(d):
        return (lax.rem(me + d + n, n), mine)

    def beside(e, d):
        return (team * group + lax.rem(seat + e, group), lax.rem(mine + d, nb))

    parts = (pl.ds(0, owned), pl.ds(owned, ghosts))
    ready = (perm, ghost_in)

    def basis_copy(part, e, d, q):
        source = ready[part].at[lax.rem(seat + e, group), q]
        target = full.at[seat, mine, q, parts[part]]
        if e == 0 and d == 0:
            return pltpu.make_async_copy(source, target, basis_recv.at[part, e, d, q])
        return remote(source, target, basis_send.at[part, e, d, q], basis_recv.at[part, e, d, q], beside(e, d))

    def basis_wait(d, q):
        for part in range(2):
            for e in range(group):
                if e == 0 and d == 0:
                    basis_copy(part, e, d, q).wait()
                    continue
                target = full.at[lax.rem(seat + group - e, group), lax.rem(mine + nb - d, nb), q, parts[part]]
                remote(ready[part].at[0, q], target, basis_send.at[part, e, d, q],
                       basis_recv.at[part, e, d, q], beside(e, d)).wait_recv()

    def basis_out(part, bands, q):
        for d in bands:
            for e in range(group):
                if e == 0 and d == 0:
                    basis_copy(part, e, d, q).start()
                else:
                    launch([basis_copy(part, e, d, q)])

    for load in loads[:3]:
        load.wait()
    owned_ids = lax.broadcasted_iota(jnp.int32, (owned, slots), 0)
    hot_parts = [
        jnp.where(owned_ids == send_ref[0, k : k + 1, :], 1.0, 0.0) for k in range(width)
    ]
    send_hot_f = jnp.concatenate(hot_parts, axis=1)
    send_hot_t = send_hot_f.astype(bf16)
    send_hot = send_hot_f.T.astype(bf16)

    mass_row = mass_ref[...]
    high = mass_row.astype(bf16).astype(f32)
    middle = (mass_row - high).astype(bf16).astype(f32)
    low = mass_row - high - middle
    level = lax.broadcasted_iota(jnp.int32, (8, owned), 0)
    extra = jnp.where(level == 0, high, jnp.where(level == 1, middle, jnp.where(level == 2, low, 0.0)))
    raised = jnp.concatenate(
        [x_ref[...].astype(f32), extra, jnp.zeros((wide - columns - 8, owned), f32)], axis=0
    ).T
    raised_f, raised = raised, raised.astype(bf16)
    first_id = columns + 3
    lane = lax.broadcasted_iota(jnp.int32, (ghosts, wide), 1)
    message = dot(send_hot, raised)
    numbers = dot(
        send_hot, (lax.broadcasted_iota(jnp.int32, (owned, wide), 0) + 1).astype(f32).astype(bf16)
    )
    for j in range(width):
        tiled = jnp.concatenate([numbers[j * slots : (j + 1) * slots]] * width, axis=0)
        message = jnp.where(lane == first_id + j, tiled, message)
    intro_out[...] = message.astype(bf16)
    mass_own = jnp.broadcast_to(mass_row, (8, owned)).T[:, :1]

    pl.semaphore_wait(barrier, len(met) + (nb - 1) * group)

    def halo(source, target, send, recv, cut):
        return [
            remote(cut(source, k), cut(target, (k + reach) % width), send.at[k], recv.at[(k + reach) % width],
                   partition(neighbour_offset(k, reach)))
            for k in range(width)
        ]

    started = []

    def launch(copies):
        for copy in copies:
            copy.start()
        started.extend(copies)

    intros = halo(intro_out, intro, intro_send, intro_recv, lambda ref, k: ref.at[pl.ds(k * slots, slots)])
    launch(intros)
    loads[3].wait()
    for s in range(group):
        for q in range(per_line):
            starts = [(s + group * (q * folds + t)) * rows for t in range(folds)]
            spans = [(a, a + left) for a in starts if left] + [(a + left, a + rows) for a in starts]
            perm[s, q] = jnp.concatenate([block[:, a:b] for a, b in spans], axis=1)
            ghost_out[s, q] = dot(send_hot, perm[s, q]).astype(bf16)
    rims = halo(ghost_out, ghost_in, gb_send, gb_recv, lambda ref, k: ref.at[:, :, pl.ds(k * slots, slots)])
    order = [lax.rem(line + 1 + i, per_line) for i in range(per_line)]
    def after_send(index):
        far = range(1, nb)
        if index == 0:
            basis_out(0, far, order[0])
            launch(rims)
            for q in order:
                basis_out(0, range(1), q)
        if index == 1:
            for copy in rims:
                copy.wait_recv()
            basis_out(1, far, order[0])
            for q in order[1:]:
                basis_out(0, far, q)
                basis_out(1, far, q)
            for q in order:
                basis_out(1, range(1), q)

    after_send(0)

    for load in loads[4:]:
        load.wait()
    fold = 128 // corners
    strips = corners // fold
    stacked = jnp.concatenate([mats_ref[:, a * 128 : (a + 1) * 128] for a in range(strips)], axis=0)
    row = lax.broadcasted_iota(jnp.int32, (cells * corners, cells * strips), 0)
    column = lax.broadcasted_iota(jnp.int32, (cells * corners, cells * strips), 1)
    picked = (row % corners) // fold * cells + row // corners == column
    spread = dot(jnp.where(picked, 1.0, 0.0).astype(bf16), stacked)
    turn = lax.broadcasted_iota(jnp.int32, (cells * corners, corners), 0) % fold
    unfolded = spread[:, :corners]
    for a in range(1, fold):
        unfolded = jnp.where(turn == a, spread[:, a * corners : (a + 1) * corners], unfolded)
    mats[...] = unfolded.astype(bf16)

    live = count_ref[0]
    total_ids = lax.broadcasted_iota(jnp.int32, (total, corners), 0)
    for c in range(cells):
        hot = jnp.where(
            jnp.logical_and(total_ids == nodes_ref[c : c + 1, :], c < live), 1.0, 0.0
        ).astype(bf16)
        part = slice(c * corners, (c + 1) * corners)
        hots[:, part] = hot
        coupled[:, part] = dot_nt(hot, mats[part, :]).astype(bf16)
    stiff[...] = dot_nt(hots[...], coupled[...]).astype(bf16)

    own_rows = dot(send_hot, stiff[:owned, :]).astype(bf16)
    for _, _, pieces in plan:
        for row, kind, k, _ in pieces:
            if kind == "own":
                stack[row : row + slots, :] = own_rows[k * slots : (k + 1) * slots]
            if kind == "back":
                stack[row : row + slots, :] = stiff[owned + k * slots : owned + (k + 1) * slots, :]
    stack[sent + ghosts :, :] = stiff[:owned, :]

    for copy in intros:
        copy.wait_recv()
    there = intro[...].astype(f32)
    turned = there.T
    mass_ghost = there[:, columns : columns + 1] + there[:, columns + 1 : columns + 2] + there[:, columns + 2 : columns + 3]
    mass = jnp.concatenate([mass_own, mass_ghost], axis=0)
    slot_lane = lax.broadcasted_iota(jnp.int32, (1, ghosts), 1)
    listed = jnp.zeros((1, ghosts), f32)
    for k in range(width):
        at = first_id + (k + reach) % width
        inside = jnp.logical_and(slot_lane >= k * slots, slot_lane < (k + 1) * slots)
        listed = jnp.where(inside, turned[at : at + 1, :], listed)
    piece_lane = lax.broadcasted_iota(jnp.int32, (slots, ghosts), 1)
    mixers = []
    for k in range(width):
        inside = jnp.logical_and(piece_lane >= k * slots, piece_lane < (k + 1) * slots)
        for j in range(width):
            column = there[k * slots : (k + 1) * slots, first_id + j : first_id + j + 1]
            mixers.append(jnp.where(jnp.logical_and(inside, column == listed), 1.0, 0.0))
    mixed = dot(jnp.concatenate(mixers, axis=0).astype(bf16), stiff[owned:, :]).astype(bf16)

    def mixed_rows(k, j):
        return mixed[(k * width + j) * slots : (k * width + j + 1) * slots]

    for _, _, pieces in plan:
        for row, kind, k, j in pieces:
            if kind == "third":
                stack[row : row + slots, :] = mixed_rows(k, j)
    for k in range(width):
        stack[sent + k * slots : sent + (k + 1) * slots, :] = mixed_rows(k, (k + reach) % width)

    def held_copies(which, e, owner):
        return [
            remote(ref.at[which, owner], ref.at[which, owner], send.at[which, e], recv.at[which, e], beside(e, 0))
            for ref, send, recv in ((held, held_send, held_recv), (edge, edge_send, edge_recv))
        ]

    def share_field(which, inner, outer):
        held[which, seat] = inner.T.astype(bf16)
        outer = outer.T
        if folded:
            outer = jnp.concatenate([outer[: columns // 2], outer[columns // 2 :]], axis=1)
        edge[which, seat] = outer.astype(bf16)
        for e in range(1, group):
            launch(held_copies(which, e, seat))

    def field(which, i):
        outer = edge[which, i]
        if folded:
            outer = jnp.concatenate([outer[:, :ghosts], outer[:, ghosts:]], axis=0)
        return jnp.concatenate([held[which, i], outer], axis=1)

    def pack(value, t):
        at = folds * left + t * (rows - left)
        ends = value[:, at : at + rows - left]
        if not packed:
            return ends
        half = columns // 2
        parts = [value[:, t * left + a : t * left + a + 128] for a in range(0, left, 128)]
        return jnp.concatenate(parts + [jnp.concatenate([ends[:half], ends[half:]], axis=1)], axis=0)

    def unpack(value):
        if not packed:
            return value
        full_parts = rows // 128
        parts = [value[a * columns : (a + 1) * columns] for a in range(full_parts)]
        rest = value[full_parts * columns :]
        parts.append(jnp.concatenate([rest[:, :64], rest[:, 64:]], axis=0))
        return jnp.concatenate(parts, axis=1)

    early = [(d, q) for q in order[:-1] for d in range(nb)] + [(0, order[-1])]
    late = [(d, order[-1]) for d in range(1, nb)]
    own_band = lax.rem(mine + nb - line // per_line, nb)
    sooner = early[:-1]
    later = [(lax.rem(own_band + 1 + i, nb), order[-1]) for i in range(nb)]

    def target_line(d, q):
        return lax.rem(mine + nb - d, nb) * per_line + q

    def cross_copy(which, d, q, f):
        to = target_line(d, q)
        there = lax.rem(side + f, folds)
        return remote(tile.at[which, to, there], across.at[which, to, f], cross_send.at[which, to, f],
                      cross_recv.at[which, to, f], ((line * folds + there) * group + seat, mine))

    def tile_copy(which, to):
        return remote(merged.at[which, to], got.at[which, line], tile_send.at[which, to],
                      tile_recv.at[which, line], ((to * folds + side) * group + seat, mine))

    def fields_in(which):
        for e in range(1, group):
            for copy in held_copies(which, e, lax.rem(seat + group - e, group)):
                copy.wait_recv()

    def begin(which, some):
        own = field(which, seat)
        return [dot(own, full[seat, lax.rem(mine + nb - d, nb), q]) for d, q in some]

    def multiply(which, some, begun=None):
        begun = begun or begin(which, some)
        others = [lax.rem(seat + e, group) for e in range(1, group)]
        fields = [field(which, i) for i in others]
        for (d, q), value in zip(some, begun):
            band, to = lax.rem(mine + nb - d, nb), target_line(d, q)
            for i, other in zip(others, fields):
                value = value + dot(other, full[i, band, q])
            for t in range(folds):
                part = pack(value, t)
                summed[which, to, t] = part
                tile[which, to, t] = part.astype(bf16)
            launch([cross_copy(which, d, q, f) for f in range(1, folds)])

    def tiles_on(which, some):
        for d, q in some:
            to = target_line(d, q)
            acc = summed[which, to, side]
            for f in range(1, folds):
                cross_copy(which, d, q, f).wait_recv()
                acc = acc + across[which, to, f].astype(f32)
            merged[which, to] = acc.astype(bf16)

            @pl.when(to != line)
            def _():
                tile_copy(which, to).start()

            @pl.when(to == line)
            def _():
                kept[which] = acc

    def tiles_in(which):
        def collect(d, acc):
            source = lax.rem(line + d, lines)
            remote(merged.at[which, source], got.at[which, source], tile_send.at[which, source],
                   tile_recv.at[which, source], ((source * folds + side) * group + seat, mine)).wait_recv()
            return acc + got[which, source].astype(f32)

        return unpack(lax.fori_loop(1, lines, collect, kept[which], unroll=lines <= 4))

    sigmas = sigma_values()
    start = jnp.concatenate([raised_f, there], axis=0)
    previous = current = jnp.concatenate(
        [start[:, :whole]] + [start[:, whole:columns]] * repeats, axis=1
    ).astype(bf16)
    strip = lax.broadcasted_iota(jnp.int32, (slots, 128), 1) // rest

    def repeat(value):
        shift = rest
        while shift < 128:
            value = value + pltpu.roll(value, shift, 1)
            shift *= 2
        return value

    for step in range(3):
        scaled = (mass * current.astype(f32)).astype(bf16)
        near_rows = plan[width][1]
        leaving = near = dot(stack[:near_rows, :], scaled)
        shift = 0
        copies = []
        base_row = 0
        for index, (d, row, pieces) in enumerate(plan):
            size = slots * len(pieces)
            if row == near_rows:
                leaving, shift = dot(stack[near_rows:sent, :], scaled), near_rows
            row -= shift
            out[step, base_row : base_row + size] = leaving[row : row + size, :whole].astype(bf16)
            ends = leaving[row : row + slots, whole:]
            for i in range(1, len(pieces)):
                ends = jnp.where(strip == i, leaving[row + i * slots : row + (i + 1) * slots, whole:], ends)
            out[step, base_row + size : base_row + size + slots, :128] = ends.astype(bf16)
            span = pl.ds(base_row, size + slots)
            copies.append(
                remote(out.at[step, span], landed.at[step, span], halo_send.at[step, index],
                       halo_recv.at[step, index], partition(d))
            )
            launch(copies[-1:])
            base_row += size + slots
        local = dot(stack[sent:, :], scaled)
        if step == 0:
            scale_now, mixing = sigmas[0] / filter_half, 0.0
        else:
            scale_now, mixing = 2.0 * sigmas[step] / filter_half, sigmas[step - 1] * sigmas[step]
        after_send(step + 1)
        base = -(filter_centre * scale_now) * current.astype(f32)
        if step > 0:
            base = base - mixing * previous.astype(f32)
        if step == 2:
            ends = {}
            for _, _, pieces in plan:
                for row, kind, k, _ in pieces:
                    if kind == "back":
                        ends[k] = near[row : row + slots]
            outer = jnp.concatenate([ends[k] for k in range(width)], axis=0)
            share_field(
                0,
                (scale_now * mass_own * local[ghosts:] + base[:owned])[:, :columns],
                (scale_now * mass_ghost * outer)[:, :columns],
            )
            for chunk in early:
                basis_wait(*chunk)
            begun = begin(0, early)
            fields_in(0)
            multiply(0, early, begun)
        for copy in copies:
            copy.wait_recv()
        arrived = landed[step].astype(f32)
        ghost_sums = [local[k * slots : (k + 1) * slots, :whole] for k in range(width)]
        ghost_ends = [jnp.zeros((slots, 128), f32)] * width
        backs, back_ends = [None] * width, [None] * width
        base_row = 0
        for _, _, pieces in plan:
            edge_row = base_row + slots * len(pieces)
            ends = arrived[edge_row : edge_row + slots, :128]
            for i, (_, kind, k, j) in enumerate(pieces):
                at = base_row + i * slots
                end = jnp.where(strip == i, ends, 0.0)
                if kind == "back":
                    backs[(k + reach) % width] = landed[step, at : at + slots]
                    back_ends[(k + reach) % width] = end
                    continue
                block_k = ((k if kind == "own" else j) + reach) % width
                ghost_sums[block_k] += arrived[at : at + slots]
                ghost_ends[block_k] += end
            base_row = edge_row + slots
        returned = jnp.concatenate(
            [jnp.concatenate(backs, axis=0), repeat(jnp.concatenate(back_ends, axis=0)).astype(bf16)], axis=1
        )
        inner = local[ghosts:] + dot(send_hot_t, returned)
        ghost_sums = [
            jnp.concatenate(
                [ghost_sums[k], local[k * slots : (k + 1) * slots, whole:] + repeat(ghost_ends[k])], axis=1
            )
            for k in range(width)
        ]
        sums = jnp.concatenate([inner] + ghost_sums, axis=0)
        previous, current = current, (scale_now * (mass * sums) + base).astype(bf16)

    scaled = (mass * current.astype(f32)).astype(bf16)
    image = mass * dot(stiff[...], scaled)
    share_field(1, image[:owned, :columns], image[owned:, :columns])
    f_ref[...] = current[:owned, :columns].astype(f32).T.astype(bf16)
    begun = begin(1, sooner)
    fields_in(1)
    multiply(1, sooner[:1], begun[:1])
    tiles_on(0, early[:1])
    multiply(1, sooner[1:], begun[1:])
    tiles_on(0, early[1:])
    for chunk in late:
        basis_wait(*chunk)
    multiply(1, later)
    multiply(0, late)
    tiles_on(1, sooner)
    tiles_on(1, later)
    tiles_on(0, late)
    ham_ref[...] = tiles_in(1)
    inter_ref[...] = tiles_in(0)

    for copy in started:
        copy.wait_send()
    for which in range(2):
        def drain(d, carry):
            tile_copy(which, lax.rem(line + d, lines)).wait_send()
            return carry

        lax.fori_loop(1, lines, drain, 0)


def deliver(*refs):
    stores = [pltpu.make_async_copy(refs[i], refs[3 + i], refs[6].at[i]) for i in range(3)]
    for store in stores:
        store.start()
    for store in stores:
        store.wait()


def on_device(n, nb, band_block, band_basis, mass_scale, cell_matrices, cell_nodes, cell_count, send_index):
    columns, owned = band_block.shape
    cell_slots, corners = cell_nodes.shape
    width, slots = send_index.shape[1:]
    cols = band_basis.shape[1]
    rows = cols * nb // n
    count = cell_slots * corners
    ghosts = width * slots
    total = owned + ghosts
    group = math.gcd(2, n // nb)
    teams = n // group
    per_seat = n // nb // group
    folds = math.gcd(2, per_seat)
    lines = teams // folds
    per_line = per_seat // folds
    wide = -(-(columns + 3 + width) // 128) * 128
    packed = rows % 128 == 64 and columns % 32 == 0
    folded = ghosts == 64 and columns % 32 == 0
    tile_shape = (columns * rows // 128, 128) if packed else (columns, rows)
    edge_shape = (columns // 2, 128) if folded else (columns, ghosts)
    _, sent, packets = routes(width // 2, slots)
    anywhere = pl.BlockSpec(memory_space=pl.ANY)
    smem = pl.BlockSpec(memory_space=pltpu.SMEM)
    semaphores = pltpu.SemaphoreType.DMA
    filtered, inter, ham = pl.pallas_call(
        functools.partial(kernel, n, nb, group, packed, folded),
        out_shape=(
            pltpu.VMEM((columns, owned), bf16),
            pltpu.VMEM((columns, rows), f32),
            pltpu.VMEM((columns, rows), f32),
        ),
        in_specs=[anywhere] * 5 + [smem, anywhere],
        out_specs=(pl.BlockSpec(memory_space=pltpu.VMEM),) * 3,
        scratch_shapes=[
            pltpu.VMEM((columns, owned), bf16),
            pltpu.VMEM((owned, cols), bf16),
            pltpu.VMEM((1, owned), f32),
            pltpu.VMEM((cell_slots, corners * corners), bf16),
            pltpu.VMEM((cell_slots, corners), jnp.int32),
            pltpu.VMEM(send_index.shape, jnp.int32),
            pltpu.VMEM((group, nb, per_line, total, folds * rows), bf16),
            pltpu.VMEM((group, per_line, owned, folds * rows), bf16),
            pltpu.VMEM((group, per_line, ghosts, folds * rows), bf16),
            pltpu.VMEM((group, per_line, ghosts, folds * rows), bf16),
            pltpu.VMEM((count, corners), bf16),
            pltpu.VMEM((total, count), bf16),
            pltpu.VMEM((total, count), bf16),
            pltpu.VMEM((total, total), bf16),
            pltpu.VMEM((sent + total, total), bf16),
            pltpu.VMEM((ghosts, wide), bf16),
            pltpu.VMEM((ghosts, wide), bf16),
            pltpu.VMEM((3, packets, columns - columns % 128), bf16),
            pltpu.VMEM((3, packets, columns - columns % 128), bf16),
            pltpu.VMEM((2, group, columns, owned), bf16),
            pltpu.VMEM((2, group) + edge_shape, bf16),
            pltpu.VMEM((2, lines, folds) + tile_shape, f32),
            pltpu.VMEM((2, lines, folds) + tile_shape, bf16),
            pltpu.VMEM((2, lines, folds) + tile_shape, bf16),
            pltpu.VMEM((2, lines) + tile_shape, bf16),
            pltpu.VMEM((2,) + tile_shape, f32),
            pltpu.VMEM((2, lines) + tile_shape, bf16),
            semaphores((6,)),
            semaphores((width,)),
            semaphores((width,)),
            semaphores((3, 2 * width)),
            semaphores((3, 2 * width)),
            semaphores((width,)),
            semaphores((width,)),
            semaphores((2, group, nb, per_line)),
            semaphores((2, group, nb, per_line)),
            semaphores((2, group)),
            semaphores((2, group)),
            semaphores((2, group)),
            semaphores((2, group)),
            semaphores((2, lines, folds)),
            semaphores((2, lines, folds)),
            semaphores((2, lines)),
            semaphores((2, lines)),
        ],
        compiler_params=pltpu.CompilerParams(collective_id=0, has_side_effects=True, vmem_limit_bytes=60 << 20),
    )(
        band_block,
        band_basis,
        mass_scale.reshape(1, owned),
        cell_matrices,
        cell_nodes,
        cell_count,
        send_index,
    )
    results = tuple(pltpu.with_memory_space_constraint(v, pltpu.VMEM) for v in (filtered, inter, ham))
    filtered, inter, ham = pl.pallas_call(
        deliver,
        out_shape=tuple(jax.ShapeDtypeStruct(v.shape, v.dtype) for v in results),
        in_specs=[pl.BlockSpec(memory_space=pltpu.VMEM)] * 3,
        out_specs=(anywhere,) * 3,
        scratch_shapes=[semaphores((3,))],
        compiler_params=pltpu.CompilerParams(vmem_limit_bytes=60 << 20),
    )(*results)
    return filtered, inter.T, ham.T


def solution(mesh):
    placed = (
        P("band", "mesh"),
        P("mesh", "band"),
        P("mesh"),
        P("mesh", None),
        P("mesh", None),
        P("mesh"),
        P("mesh", None, None),
    )
    return jax.shard_map(
        functools.partial(on_device, mesh.shape["mesh"], mesh.shape["band"]),
        mesh=mesh,
        in_specs=placed,
        out_specs=(P("band", "mesh"), P("mesh", "band"), P("mesh", "band")),
        check_vma=False,
    )
```
